32 devices in a mesh: group: 8 (over z, x), owner: 4 (over y, core).
Axes of the slice: x: 2, y: 2, z: 4, core: 2. Of those that a mesh axis runs over, the one named last changes fastest.
Arguments:
- embeddings: bfloat16 [32768, 1024], P(('group', 'owner')), may hold values from -2 to 2
- home_pairs: int32 [8, 4, 3, 64, 2], P('group', 'owner'), may hold values from 0 to 7, as said below
- home_count: int32 [8, 4, 3], P('group', 'owner'), may hold values from 0 to 28
- surplus_pairs: int32 [8, 4, 8, 3], P('group', 'owner'), may hold values from 0 to 7, as said below
Outputs:
- centered: bfloat16 [32768, 1024], P(('group', 'owner'))
- log_density: float32 [32768], P(('group', 'owner'))
The draws below stay inside these ranges and needn't reach their ends.
Inputs may be any that keep to these rules, and one draw needn't show every extreme that they name: `home_pairs`: for owner o of group g and distance s, the first home_count[g, o, s] slots hold distinct pairs (a, b) of block a of owner o and block b of owner (o + s) mod 4 that lie in one cluster; at distance 0 a <= b and every pair (a, a) is listed; at twice s equal to 4 only owners below 2 list pairs; later slots are ignored. `surplus_pairs`: A live entry (a, b, 1) names two blocks of the same owner in one cluster with a < b; no pair is live twice or also listed in home_pairs; dead entries are ignored.
All inputs are finite; a program needn't handle non-finite values.
Results may differ from the reference program's by a relative error of at most 0.0057.
Values may be sent and summed in bfloat16 or wider, within the bound.
A program may use at most 128 MiB of HBM per device.

```python
import jax
import jax.numpy as jnp
from jax import lax

D = 1024
BLOCK = 128
BPD = 8
SHIFTS = 3
SLOTS = 64
ROWS = 32768
N_GROUP = 8
N_OWNER = 4


topic_count = 16


def offset_ranks(group_total):
    half_way = group_total // 2
    leading = [half_way, 1, group_total - 1, half_way + 1, half_way - 1, 2]
    others = [offset for offset in range(1, group_total) if offset not in leading]
    ordered = leading + others + [0]
    table = [0] * group_total
    for place in range(group_total):
        table[ordered[place]] = place
    return jnp.array(table, dtype=jnp.int32)


def pair_plan(base_key):
    sub_keys = jax.random.split(jax.random.fold_in(base_key, 7), 2)
    heavy_owner = jax.random.randint(sub_keys[0], (N_GROUP, 1, 1), 0, N_OWNER, jnp.int32)
    light_ids = jax.random.randint(sub_keys[1], (N_GROUP, N_OWNER, BPD), 1, 1 + 6 * BPD, jnp.int32)
    owner_ids = jnp.arange(N_OWNER, dtype=jnp.int32)
    cluster = jnp.where(owner_ids[None, :, None] == heavy_owner, 0, light_ids).astype(jnp.int32)
    distance = jnp.arange(SHIFTS, dtype=jnp.int32)
    partner = (owner_ids[:, None] + distance[None, :]) % N_OWNER
    partner_cluster = cluster[:, partner]
    same_cluster = cluster[:, :, None, :, None] == partner_cluster[:, :, :, None, :]
    block_ids = jnp.arange(BPD, dtype=jnp.int32)
    upper_tri = block_ids[:, None] <= block_ids[None, :]
    strict_upper = block_ids[:, None] < block_ids[None, :]
    at_zero = (distance == 0)[None, None, :, None, None]
    at_half = (2 * distance == N_OWNER)[None, None, :, None, None]
    low_owner = (owner_ids < N_OWNER // 2)[None, :, None, None, None]
    allowed = jnp.where(at_zero, upper_tri[None, None, None], True) & (jnp.logical_not(at_half) | low_owner)
    candidate = (same_cluster & allowed).reshape(N_GROUP, N_OWNER, SHIFTS, SLOTS)
    off_pairs = (same_cluster[:, :, 0] & strict_upper).reshape(N_GROUP, N_OWNER, SLOTS)
    rank = jnp.cumsum(off_pairs.astype(jnp.int32), axis=-1) - 1
    shipped = off_pairs & (rank < N_GROUP)
    home_zero = candidate[:, :, 0] & jnp.logical_not(shipped)
    home = candidate.at[:, :, 0].set(home_zero)
    positions = jnp.arange(SLOTS, dtype=jnp.int32)
    home_key = (1 - home.astype(jnp.int32)) * SLOTS + positions
    home_order = jnp.argsort(home_key, axis=-1, stable=True).astype(jnp.int32)
    home_pairs = jnp.stack([home_order // BPD, home_order % BPD], axis=-1).astype(jnp.int32)
    home_count = jnp.sum(home.astype(jnp.int32), axis=-1, dtype=jnp.int32)
    off_key = (1 - off_pairs.astype(jnp.int32)) * SLOTS + positions
    off_order = jnp.argsort(off_key, axis=-1, stable=True).astype(jnp.int32)
    off_count = jnp.sum(off_pairs.astype(jnp.int32), axis=-1, dtype=jnp.int32)
    group_ids = jnp.arange(N_GROUP, dtype=jnp.int32)
    rank_table_small = offset_ranks(N_GROUP)
    slot_rank = rank_table_small[(group_ids[None, :] - group_ids[:, None]) % N_GROUP]
    rank_table = jnp.broadcast_to(slot_rank[:, None, :], (N_GROUP, N_OWNER, N_GROUP))
    picked = jnp.take_along_axis(off_order, rank_table, axis=-1)
    live_flag = (rank_table < off_count[..., None]).astype(jnp.int32)
    surplus = jnp.stack([picked // BPD, picked % BPD, live_flag], axis=-1).astype(jnp.int32)
    return (home_pairs, home_count, surplus)


def draw_home_pairs(key, part):
    return pair_plan(key)[0]


def draw_home_count(key, part):
    return pair_plan(key)[1]


def draw_surplus_pairs(key, part):
    return pair_plan(key)[2]


def draw_embeddings(key, part):
    sub_keys = jax.random.split(jax.random.fold_in(key, 3), 4)
    centers = jax.random.normal(sub_keys[0], (topic_count, D), jnp.float32)
    topics = jax.random.randint(sub_keys[1], (ROWS,), 0, topic_count, jnp.int32)
    noise = jax.random.normal(sub_keys[2], (ROWS, D), jnp.float32)
    spread = jax.random.uniform(sub_keys[3], (ROWS, 1), jnp.float32, 0.4, 1.6)
    vectors = centers[topics] + spread * noise
    return jnp.clip(0.25 * vectors, -2.0, 2.0).astype(jnp.bfloat16)


def setup_inputs(seed: int = 0) -> dict:
    seeds = jax.random.split(jax.random.key(seed), 5)
    return {
        "embeddings": draw_embeddings(jax.random.fold_in(seeds[4], 71), 0),
        "home_pairs": draw_home_pairs(jax.random.fold_in(seeds[4], 71), 0),
        "home_count": draw_home_count(jax.random.fold_in(seeds[4], 71), 0),
        "surplus_pairs": draw_surplus_pairs(jax.random.fold_in(seeds[4], 71), 0),
    }


sharpness = 4.0
epsilon = 1e-06
batch_pairs = 16

def unit_rows(embeddings):
    widened = embeddings.astype(jnp.float32)
    inv_rms = lax.rsqrt(lax.optimization_barrier(jnp.mean(widened * widened, axis=-1, keepdims=True)) + epsilon)
    return (widened * inv_rms).astype(jnp.bfloat16)

def round_half(value):
    return lax.optimization_barrier(value.astype(jnp.bfloat16)).astype(jnp.float32)

def pair_terms(first_block, second_block):
    first_wide = first_block.astype(jnp.float32)
    second_wide = second_block.astype(jnp.float32)
    embed_width = first_block.shape[-1]
    similarity = jnp.einsum('nid,njd->nij', first_wide, second_wide) * (1.0 / embed_width)
    kernel = jnp.exp(sharpness * (similarity - 1.0))
    kernel_low = round_half(kernel)
    to_first = jnp.einsum('nij,njd->nid', kernel_low, second_wide)
    to_second = jnp.einsum('nij,nid->njd', kernel_low, first_wide)
    return (to_first, to_second, lax.optimization_barrier(jnp.sum(kernel, axis=2)), lax.optimization_barrier(jnp.sum(kernel, axis=1)))

def add_pairs(blocks, first_ids, second_ids, live_mask, second_scale, round_terms, totals):
    pad_ids = jnp.zeros((batch_pairs,), jnp.int32)
    first_ids = jnp.concatenate([first_ids.astype(jnp.int32), pad_ids])
    second_ids = jnp.concatenate([second_ids.astype(jnp.int32), pad_ids])
    live_mask = jnp.concatenate([live_mask.astype(jnp.int32), pad_ids])
    second_scale = jnp.concatenate([second_scale.astype(jnp.float32), jnp.zeros((batch_pairs,), jnp.float32)])
    live_first = jnp.argsort(1 - live_mask, stable=True).astype(jnp.int32)
    live_count = jnp.sum(live_mask, dtype=jnp.int32)

    def step(turn_index, carry):
        near_sums, near_dens, far_sums, far_dens = carry
        picked = lax.dynamic_slice_in_dim(live_first, turn_index * batch_pairs, batch_pairs, 0)
        positions = turn_index * batch_pairs + jnp.arange(batch_pairs, dtype=jnp.int32)
        keep_mask = (positions < live_count).astype(jnp.float32)
        first_pick = first_ids[picked]
        second_pick = second_ids[picked]
        to_first, to_second, dens_first, dens_second = pair_terms(blocks[first_pick], blocks[second_pick])
        if round_terms:
            to_first = round_half(to_first)
            to_second = round_half(to_second)
            dens_first = round_half(dens_first)
            dens_second = round_half(dens_second)
        other_mask = keep_mask * second_scale[picked]
        near_sums = near_sums.at[first_pick].add(to_first * keep_mask[:, None, None])
        near_dens = near_dens.at[first_pick].add(dens_first * keep_mask[:, None])
        far_sums = far_sums.at[second_pick].add(to_second * other_mask[:, None, None])
        far_dens = far_dens.at[second_pick].add(dens_second * other_mask[:, None])
        return (near_sums, near_dens, far_sums, far_dens)
    turn_count = (live_count + batch_pairs - 1) // batch_pairs
    return lax.fori_loop(0, turn_count, step, totals)

def reference(embeddings, home_pairs, home_count, surplus_pairs):
    normed = unit_rows(embeddings)
    embed_width = normed.shape[1]
    blocks = normed.reshape(-1, BLOCK, embed_width)
    block_count = blocks.shape[0]
    near_sums = jnp.zeros((block_count, BLOCK, embed_width), jnp.float32)
    near_dens = jnp.zeros((block_count, BLOCK), jnp.float32)
    groups = jnp.arange(N_GROUP, dtype=jnp.int32)[:, None, None]
    owners = jnp.arange(N_OWNER, dtype=jnp.int32)[None, :, None]
    slot_ids = jnp.arange(SLOTS, dtype=jnp.int32)[None, None, :]
    for distance in range(N_OWNER // 2 + 1):
        pair_list = home_pairs[:, :, distance]
        partner = (owners + distance) % N_OWNER
        first_ids = ((groups * N_OWNER + owners) * BPD + pair_list[..., 0]).reshape(-1)
        second_ids = ((groups * N_OWNER + partner) * BPD + pair_list[..., 1]).reshape(-1)
        live_mask = (slot_ids < home_count[:, :, distance][..., None]).astype(jnp.int32).reshape(-1)
        if distance == 0:
            second_scale = (first_ids != second_ids).astype(jnp.float32)
        else:
            second_scale = jnp.ones(first_ids.shape, jnp.float32)
        far_sums = jnp.zeros_like(near_sums)
        far_dens = jnp.zeros_like(near_dens)
        near_sums, near_dens, far_sums, far_dens = add_pairs(blocks, first_ids, second_ids, live_mask, second_scale, False, (near_sums, near_dens, far_sums, far_dens))
        if distance == 0:
            near_sums = near_sums + far_sums
            near_dens = near_dens + far_dens
        else:
            near_sums = near_sums + round_half(far_sums)
            near_dens = near_dens + round_half(far_dens)
    first_ids = ((groups * N_OWNER + owners) * BPD + surplus_pairs[..., 0]).reshape(-1)
    second_ids = ((groups * N_OWNER + owners) * BPD + surplus_pairs[..., 1]).reshape(-1)
    live_mask = surplus_pairs[..., 2].reshape(-1)
    second_scale = jnp.ones(first_ids.shape, jnp.float32)
    far_sums = jnp.zeros_like(near_sums)
    far_dens = jnp.zeros_like(near_dens)
    near_sums, near_dens, far_sums, far_dens = add_pairs(blocks, first_ids, second_ids, live_mask, second_scale, True, (near_sums, near_dens, far_sums, far_dens))
    near_sums = near_sums + far_sums
    near_dens = near_dens + far_dens
    log_density = jnp.log(near_dens).reshape(-1)
    centered = (blocks.astype(jnp.float32) - near_sums / near_dens[..., None]).astype(jnp.bfloat16)
    return (centered.reshape(-1, embed_width), log_density)
```

```python
import functools

import jax
import jax.numpy as jnp
from jax import lax
from jax.experimental import pallas as pl
from jax.experimental.pallas import tpu as pltpu
from jax.sharding import PartitionSpec as P

BLOCK = 128
LANES = 128
VMEM_BYTES = 56 * 1024 * 1024

sharpness = 4.0
epsilon = 1e-06

VMEM = pltpu.MemorySpace.VMEM
SMEM = pltpu.MemorySpace.SMEM
ANY = pl.ANY


def kernel_of(first, second):
    width = first.shape[-1]
    similarity = lax.dot_general(
        first, second, (((1,), (1,)), ((), ())), preferred_element_type=jnp.float32
    ) * (1.0 / width)
    return jnp.exp(sharpness * (similarity - 1.0))


def prep_kernel(shifts, surplus, lists_ref, emb_ref, unit_ref, mask_ref):
    blocks = unit_ref.shape[0]
    mask_ref[...] = jnp.zeros_like(mask_ref)
    one = jnp.ones((1, BLOCK), jnp.float32)

    def mark(a, b):
        mask_ref[a, :, pl.ds(pl.multiple_of(b * BLOCK, BLOCK), BLOCK)] = one
        mask_ref[b, :, pl.ds(pl.multiple_of(a * BLOCK, BLOCK), BLOCK)] = one

    @pl.loop(0, lists_ref[shifts, 0])
    def _(t):
        mark(lists_ref[0, 2 * t], lists_ref[0, 2 * t + 1])

    @pl.loop(0, surplus)
    def _(t):
        @pl.when(lists_ref[2 * shifts, 3 * t + 2] == 1)
        def _():
            mark(lists_ref[2 * shifts, 3 * t], lists_ref[2 * shifts, 3 * t + 1])

    @pl.loop(0, blocks)
    def _(i):
        wide = emb_ref[i].astype(jnp.float32)
        inv = lax.rsqrt(jnp.mean(wide * wide, axis=-1, keepdims=True) + epsilon)
        unit_ref[i] = (wide * inv).astype(jnp.bfloat16)


def exchange_kernel(
    n, unit_ref, lists_ref, mask_ref, recv_ref, all_lists_ref, acc_ref, dens_ref,
    send_sem, recv_sem, side_send, side_recv, fwd_send, fwd_recv, list_send, list_recv,
):
    me = lax.axis_index("owner")
    blocks = unit_ref.shape[0]
    width = unit_ref.shape[2]
    chips = n // 2
    sibling = me + 1 - 2 * lax.rem(me, 2)

    barrier = pltpu.get_barrier_semaphore()
    for d in range(1, n):
        pl.semaphore_signal(barrier, inc=1, device_id={"owner": lax.rem(me + d, n)})
    pl.semaphore_wait(barrier, n - 1)

    def list_copy(d):
        return pltpu.make_async_remote_copy(
            src_ref=lists_ref, dst_ref=all_lists_ref.at[me],
            send_sem=list_send.at[d], recv_sem=list_recv.at[d],
            device_id={"owner": lax.rem(me + d, n)},
        )

    def cross_copy(k, i):
        return pltpu.make_async_remote_copy(
            src_ref=unit_ref.at[i], dst_ref=recv_ref.at[me, i],
            send_sem=send_sem.at[k, i], recv_sem=recv_sem.at[k, i],
            device_id={"owner": lax.rem(me + 2 * k, n)},
        )

    def forward_copy(k, i):
        source = lax.rem(me + n - 2 * k, n)
        return pltpu.make_async_remote_copy(
            src_ref=recv_ref.at[source, i], dst_ref=recv_ref.at[source, i],
            send_sem=fwd_send.at[k, i], recv_sem=fwd_recv.at[k, i],
            device_id={"owner": sibling},
        )

    side = pltpu.make_async_remote_copy(
        src_ref=unit_ref, dst_ref=recv_ref.at[me],
        send_sem=side_send, recv_sem=side_recv, device_id={"owner": sibling},
    )

    for d in range(1, n):
        list_copy(d).start()
    for k in range(1, chips):
        for i in range(blocks):
            cross_copy(k, i).start()
    side.start()

    every = unit_ref[...].reshape(blocks * BLOCK, width)

    @pl.loop(0, blocks // 2)
    def _(c):
        rows = unit_ref[pl.ds(2 * c, 2)].reshape(2 * BLOCK, width)
        upper = jnp.broadcast_to(mask_ref[2 * c], (BLOCK, blocks * BLOCK))
        lower = jnp.broadcast_to(mask_ref[2 * c + 1], (BLOCK, blocks * BLOCK))
        weights = kernel_of(rows, every) * jnp.concatenate([upper, lower], axis=0)
        total = jnp.sum(weights, axis=1, keepdims=True)
        dens_ref[pl.ds(2 * c, 2)] = jnp.broadcast_to(total, (2 * BLOCK, LANES)).reshape(2, BLOCK, LANES)
        near = jnp.dot(weights.astype(jnp.bfloat16), every, preferred_element_type=jnp.float32)
        acc_ref[pl.ds(2 * c, 2)] = near.reshape(2, BLOCK, width)

    for i in range(blocks):
        for k in range(1, chips):
            cross_copy(k, i).wait_recv()
            forward_copy(k, i).start()
    side.wait()
    for d in range(1, n):
        list_copy(d).wait()
    for i in range(blocks):
        for k in range(1, chips):
            cross_copy(k, i).wait_send()
            forward_copy(k, i).wait()


def far_kernel(
    n, shifts, rows, lists_ref, all_lists_ref, unit_ref, acc_in, dens_in, recv_ref,
    out_ref, log_ref, acc_ref, dens_ref, near_ids, far_ids, held, sems, copy_sem,
):
    me = lax.axis_index("owner")
    blocks = unit_ref.shape[0]
    width = unit_ref.shape[2]

    def add(total, near, far):
        near_ids[total] = near
        far_ids[total] = far

    total = jnp.int32(0)
    for s in range(1, shifts):
        ahead = lax.rem(me + s, n)
        behind = lax.rem(me + n - s, n)
        count = lists_ref[shifts + s, 0]

        @pl.loop(0, count)
        def _(t, total=total, ahead=ahead, s=s):
            add(total + t, lists_ref[s, 2 * t], ahead * blocks + lists_ref[s, 2 * t + 1])

        total = total + count
        count = all_lists_ref[behind * rows + shifts + s, 0]

        @pl.loop(0, count)
        def _(t, total=total, behind=behind, s=s):
            row = behind * rows + s
            add(total + t, all_lists_ref[row, 2 * t + 1], behind * blocks + all_lists_ref[row, 2 * t])

        total = total + count

    def fetch(t):
        return pltpu.make_async_copy(recv_ref.at[far_ids[t]], held.at[lax.rem(t, 2)], sems.at[lax.rem(t, 2)])

    @pl.when(total > 0)
    def _():
        fetch(0).start()

    acc_ref[...] = acc_in[...]
    dens_ref[...] = dens_in[...]

    @pl.loop(0, total)
    def _(t):
        @pl.when(t + 1 < total)
        def _():
            fetch(t + 1).start()

        fetch(t).wait()
        a = near_ids[t]
        other = held[lax.rem(t, 2)]
        weights = kernel_of(unit_ref[a], other)
        dens_ref[a] += jnp.broadcast_to(jnp.sum(weights, axis=1, keepdims=True), (BLOCK, LANES))
        acc_ref[a] += jnp.dot(weights.astype(jnp.bfloat16), other, preferred_element_type=jnp.float32)

    @pl.loop(0, blocks)
    def _(i):
        dens = dens_ref[i]
        share = acc_ref[i] / dens[:, 0:1]
        out_ref[i] = (unit_ref[i].astype(jnp.float32) - share).astype(jnp.bfloat16)
        log_ref[i] = jnp.log(dens.T[0:1])


def shards(embeddings, home_pairs, home_count, surplus_pairs):
    n = lax.axis_size("owner")
    width = embeddings.shape[1]
    blocks = embeddings.shape[0] // BLOCK
    shifts = home_pairs.shape[2]
    slots = home_pairs.shape[3]
    surplus = surplus_pairs.shape[2]
    lanes = 2 * slots
    rows = -(-(2 * shifts + 1) // 8) * 8

    extra = surplus_pairs[0, 0].reshape(1, -1)
    lists = jnp.concatenate(
        [
            home_pairs[0, 0].reshape(shifts, lanes),
            jnp.broadcast_to(home_count[0, 0][:, None], (shifts, lanes)),
            jnp.pad(extra, ((0, rows - 2 * shifts - 1), (0, lanes - extra.shape[1]))),
        ],
        axis=0,
    )
    emb = embeddings.reshape(blocks, BLOCK, width)
    vmem = pl.BlockSpec(memory_space=VMEM)
    smem = pl.BlockSpec(memory_space=SMEM)
    anyw = pl.BlockSpec(memory_space=ANY)
    shape = jax.ShapeDtypeStruct

    unit, mask = pl.pallas_call(
        functools.partial(prep_kernel, shifts, surplus),
        out_shape=(
            shape((blocks, BLOCK, width), jnp.bfloat16),
            shape((blocks, 1, blocks * BLOCK), jnp.float32),
        ),
        in_specs=[smem, vmem],
        out_specs=(vmem, vmem),
        compiler_params=pltpu.CompilerParams(vmem_limit_bytes=VMEM_BYTES),
    )(lists, emb)

    chips = n // 2
    dma = pltpu.SemaphoreType.DMA
    recv, all_lists, acc, dens = pl.pallas_call(
        functools.partial(exchange_kernel, n),
        out_shape=(
            shape((n, blocks, BLOCK, width), jnp.bfloat16),
            shape((n, rows, lanes), jnp.int32),
            shape((blocks, BLOCK, width), jnp.float32),
            shape((blocks, BLOCK, LANES), jnp.float32),
        ),
        in_specs=[vmem, anyw, vmem],
        out_specs=(anyw, anyw, vmem, vmem),
        scratch_shapes=[
            dma((chips, blocks)), dma((chips, blocks)), dma, dma,
            dma((chips, blocks)), dma((chips, blocks)), dma((n,)), dma((n,)),
        ],
        compiler_params=pltpu.CompilerParams(
            collective_id=0, has_side_effects=True, vmem_limit_bytes=VMEM_BYTES
        ),
    )(unit, lists, mask)

    entries = 2 * shifts * slots
    centered, log_density = pl.pallas_call(
        functools.partial(far_kernel, n, shifts, rows),
        out_shape=(
            shape((blocks, BLOCK, width), jnp.bfloat16),
            shape((blocks, 1, BLOCK), jnp.float32),
        ),
        in_specs=[smem, smem, vmem, vmem, vmem, anyw],
        out_specs=(vmem, vmem),
        scratch_shapes=[
            pltpu.VMEM((blocks, BLOCK, width), jnp.float32),
            pltpu.VMEM((blocks, BLOCK, LANES), jnp.float32),
            pltpu.SMEM((entries,), jnp.int32),
            pltpu.SMEM((entries,), jnp.int32),
            pltpu.VMEM((2, BLOCK, width), jnp.bfloat16),
            dma((2,)),
            dma,
        ],
        compiler_params=pltpu.CompilerParams(vmem_limit_bytes=VMEM_BYTES),
    )(lists, all_lists.reshape(n * rows, lanes), unit, acc, dens, recv.reshape(n * blocks, BLOCK, width))
    return (centered.reshape(-1, width), log_density.reshape(-1))


def solution(mesh):
    return jax.shard_map(
        shards,
        mesh=mesh,
        in_specs=(
            P(("group", "owner"), None),
            P("group", "owner", None, None, None),
            P("group", "owner", None),
            P("group", "owner", None, None),
        ),
        out_specs=(P(("group", "owner"), None), P(("group", "owner"))),
        check_vma=False,
    )
```

```python
import functools

import jax
import jax.numpy as jnp
from jax import lax
from jax.experimental import pallas as pl
from jax.experimental.pallas import tpu as pltpu
from jax.sharding import PartitionSpec as P

BLOCK = 128
LANES = 128
VMEM_BYTES = 56 * 1024 * 1024

sharpness = 4.0
epsilon = 1e-06

VMEM = pltpu.MemorySpace.VMEM
SMEM = pltpu.MemorySpace.SMEM
ANY = pl.ANY


def kernel_of(first, second):
    width = first.shape[-1]
    similarity = lax.dot_general(
        first, second, (((1,), (1,)), ((), ())), preferred_element_type=jnp.float32
    ) * (1.0 / width)
    return jnp.exp(sharpness * (similarity - 1.0))


CAPACITIES = (2, 3, 4, 5, 6)


def capacity_index(peak, blocks):
    index = jnp.int32(0)
    for capacity in CAPACITIES:
        index = index + jnp.where(peak > 2 * min(capacity, blocks), 1, 0).astype(jnp.int32)
    return index


def capacity_of(peak, blocks):
    capacity = jnp.int32(blocks)
    for smaller in reversed(CAPACITIES):
        capacity = jnp.where(peak <= 2 * min(smaller, blocks), min(smaller, blocks), capacity)
    return capacity


def normalize(source_ref, target_ref, i):
    wide = source_ref[i].astype(jnp.float32)
    inv = lax.rsqrt(jnp.mean(wide * wide, axis=-1, keepdims=True) + epsilon)
    target_ref[i] = (wide * inv).astype(jnp.bfloat16)


def plan_kernel(
    n, groups, shifts, lists_ref, emb_ref, unit_ref, side_ref, need_ref, peak_ref, all_lists_ref,
    emb_side, tile, tiles, peak_tile, peaks,
    side_send, side_recv, list_send, list_recv, tile_send, tile_recv, peak_send, peak_recv,
):
    group = lax.axis_index("group")
    me = lax.axis_index("owner")
    blocks = unit_ref.shape[0]
    lanes = lists_ref.shape[1]
    sibling = me + 1 - 2 * lax.rem(me, 2)

    lane = lax.broadcasted_iota(jnp.int32, (blocks, lanes), 1)
    block = lax.broadcasted_iota(jnp.int32, (blocks, lanes), 0)
    owner_lane = lax.broadcasted_iota(jnp.int32, (blocks, LANES), 1)
    need = jnp.zeros((blocks, LANES), jnp.float32)
    for s in range(1, shifts):
        partner = lax.rem(me + s, n)
        apart = lax.div(partner, 2) != lax.div(me, 2)
        listed = jnp.broadcast_to(lists_ref[pl.ds(s, 1)], (blocks, lanes))
        count = jnp.broadcast_to(lists_ref[pl.ds(shifts + s, 1)], (blocks, lanes))
        hit = jnp.where((listed == block) & (lax.div(lane, 2) < count), 1.0, 0.0)
        first = jnp.max(jnp.where(lax.rem(lane, 2) == 0, hit, 0.0), axis=1, keepdims=True)
        second = jnp.max(jnp.where(lax.rem(lane, 2) == 1, hit, 0.0), axis=1, keepdims=True)
        scale = jnp.where(apart, 1.0, 0.0)
        need = jnp.maximum(need, jnp.where(owner_lane == me, first, 0.0) * scale)
        need = jnp.maximum(need, jnp.where(owner_lane == partner, second, 0.0) * scale)
    tile[...] = need

    barrier = pltpu.get_barrier_semaphore()
    for d in range(1, n):
        pl.semaphore_signal(barrier, inc=1, device_id={"owner": lax.rem(me + d, n)})
    for d in range(1, groups):
        pl.semaphore_signal(barrier, inc=1, device_id={"group": lax.rem(group + d, groups)})
    pl.semaphore_wait(barrier, n + groups - 2)

    def to_owner(source, target, send, recv, d):
        return pltpu.make_async_remote_copy(
            src_ref=source, dst_ref=target.at[d], send_sem=send.at[d], recv_sem=recv.at[d],
            device_id={"owner": lax.rem(me + d, n)},
        )

    def list_copy(d):
        return pltpu.make_async_remote_copy(
            src_ref=lists_ref, dst_ref=all_lists_ref.at[me],
            send_sem=list_send.at[d], recv_sem=list_recv.at[d],
            device_id={"owner": lax.rem(me + d, n)},
        )

    def peak_copy(d):
        return pltpu.make_async_remote_copy(
            src_ref=peak_tile, dst_ref=peaks.at[d], send_sem=peak_send.at[d], recv_sem=peak_recv.at[d],
            device_id={"group": lax.rem(group + d, groups)},
        )

    for d in range(1, n):
        to_owner(tile, tiles, tile_send, tile_recv, d).start()
    side = pltpu.make_async_remote_copy(
        src_ref=emb_ref, dst_ref=emb_side, send_sem=side_send, recv_sem=side_recv,
        device_id={"owner": sibling},
    )
    side.start()
    for d in range(1, n):
        list_copy(d).start()

    @pl.loop(0, blocks)
    def _(i):
        normalize(emb_ref, unit_ref, i)

    for d in range(1, n):
        to_owner(tile, tiles, tile_send, tile_recv, d).wait()
    need = tile[...]
    for d in range(1, n):
        need = jnp.maximum(need, tiles[d])
    need_ref[...] = need.astype(jnp.int32)
    peak = jnp.zeros((1, 1), jnp.float32)
    for chip in range(n // 2):
        on_chip = jnp.where(lax.div(owner_lane, 2) == chip, need, 0.0)
        total = jnp.sum(jnp.sum(on_chip, axis=1, keepdims=True), axis=0, keepdims=True)
        peak = jnp.maximum(peak, total)
    peak_tile[...] = jnp.broadcast_to(peak, peak_tile.shape)

    side.wait()
    half = blocks // 2

    @pl.loop(0, half)
    def _(i):
        normalize(emb_side, side_ref, i)

    for d in range(1, groups):
        peak_copy(d).start()

    @pl.loop(half, blocks)
    def _(i):
        normalize(emb_side, side_ref, i)

    for d in range(1, groups):
        peak_copy(d).wait()
    highest = peak_tile[...]
    for d in range(1, groups):
        highest = jnp.maximum(highest, peaks[d])
    peak_ref[...] = highest.astype(jnp.int32)
    for d in range(1, n):
        list_copy(d).wait()


def pack_kernel(n, shifts, surplus, lists_ref, need_ref, peak_ref, unit_ref, side_ref, packed_ref, mask_ref, sems):
    me = lax.axis_index("owner")
    core = lax.rem(me, 2)
    blocks = packed_ref.shape[0]
    capacity = capacity_of(peak_ref[0, 0], blocks)

    rank = jnp.int32(0)
    taken = []
    for half in range(2):
        owner = me - core + half
        for b in range(blocks):
            needed = need_ref[b, owner] == 1
            slot = rank - core * capacity
            ours = needed & (slot >= 0) & (slot < capacity)
            for own in (True, False):
                source = unit_ref if own else side_ref
                chosen = ours & ((core == half) == own)
                place = jnp.clip(slot, 0, blocks - 1)
                copy = pltpu.make_async_copy(source.at[b], packed_ref.at[place], sems.at[half, b])

                @pl.when(chosen)
                def _(copy=copy):
                    copy.start()

                taken.append((chosen, copy))
            rank = rank + needed.astype(jnp.int32)

    mask_ref[...] = jnp.zeros_like(mask_ref)
    one = jnp.ones((1, BLOCK), jnp.float32)

    def mark(a, b):
        mask_ref[a, :, pl.ds(pl.multiple_of(b * BLOCK, BLOCK), BLOCK)] = one
        mask_ref[b, :, pl.ds(pl.multiple_of(a * BLOCK, BLOCK), BLOCK)] = one

    @pl.loop(0, lists_ref[shifts, 0])
    def _(t):
        mark(lists_ref[0, 2 * t], lists_ref[0, 2 * t + 1])

    @pl.loop(0, surplus)
    def _(t):
        @pl.when(lists_ref[2 * shifts, 3 * t + 2] == 1)
        def _():
            mark(lists_ref[2 * shifts, 3 * t], lists_ref[2 * shifts, 3 * t + 1])

    for chosen, copy in taken:
        @pl.when(chosen)
        def _(copy=copy):
            copy.wait()


def exchange_kernel(
    n, capacity, packed_ref, unit_ref, mask_ref, recv_ref, acc_ref, dens_ref,
    send_sem, recv_sem, fwd_send, fwd_recv,
):
    me = lax.axis_index("owner")
    blocks = unit_ref.shape[0]
    width = unit_ref.shape[2]
    chips = n // 2
    chip = lax.div(me, 2)
    core = lax.rem(me, 2)
    sibling = me + 1 - 2 * core

    barrier = pltpu.get_barrier_semaphore()
    pl.semaphore_signal(barrier, inc=1, device_id={"owner": sibling})
    for k in range(1, chips):
        pl.semaphore_signal(barrier, inc=1, device_id={"owner": lax.rem(me + 2 * k, n)})
    pl.semaphore_wait(barrier, chips)

    def cross_copy(k, i):
        return pltpu.make_async_remote_copy(
            src_ref=packed_ref.at[i], dst_ref=recv_ref.at[chip, core * capacity + i],
            send_sem=send_sem.at[k, i], recv_sem=recv_sem.at[k, i],
            device_id={"owner": lax.rem(me + 2 * k, n)},
        )

    def forward_copy(k, i):
        source = lax.rem(chip + chips - k, chips)
        landed = recv_ref.at[source, core * capacity + i]
        return pltpu.make_async_remote_copy(
            src_ref=landed, dst_ref=landed,
            send_sem=fwd_send.at[k, i], recv_sem=fwd_recv.at[k, i],
            device_id={"owner": sibling},
        )

    for i in range(capacity):
        for k in range(1, chips):
            cross_copy(k, i).start()

    every = unit_ref[...].reshape(blocks * BLOCK, width)

    @pl.loop(0, blocks // 2)
    def _(c):
        rows = unit_ref[pl.ds(2 * c, 2)].reshape(2 * BLOCK, width)
        upper = jnp.broadcast_to(mask_ref[2 * c], (BLOCK, blocks * BLOCK))
        lower = jnp.broadcast_to(mask_ref[2 * c + 1], (BLOCK, blocks * BLOCK))
        weights = kernel_of(rows, every) * jnp.concatenate([upper, lower], axis=0)
        total = jnp.sum(weights, axis=1, keepdims=True)
        dens_ref[pl.ds(2 * c, 2)] = jnp.broadcast_to(total, (2 * BLOCK, LANES)).reshape(2, BLOCK, LANES)
        near = jnp.dot(weights.astype(jnp.bfloat16), every, preferred_element_type=jnp.float32)
        acc_ref[pl.ds(2 * c, 2)] = near.reshape(2, BLOCK, width)

    for i in range(capacity):
        for k in range(1, chips):
            cross_copy(k, i).wait_recv()
            forward_copy(k, i).start()
    for i in range(capacity):
        for k in range(1, chips):
            cross_copy(k, i).wait_send()
            forward_copy(k, i).wait()


def far_kernel(
    n, shifts, rows, lists_ref, all_lists_ref, need_ref, unit_ref, acc_in, dens_in, side_ref, recv_ref,
    out_ref, log_ref, acc_ref, dens_ref, near_ids, far_ids, places, held, sems,
):
    me = lax.axis_index("owner")
    blocks = unit_ref.shape[0]
    width = unit_ref.shape[2]
    chip = lax.div(me, 2)
    pool = 2 * blocks

    for source in range(n // 2):
        rank = jnp.int32(0)
        for half in range(2):
            for b in range(blocks):
                owner = 2 * source + half
                places[owner * blocks + b] = source * pool + rank
                rank = rank + need_ref[b, owner]

    def add(total, near, owner, b):
        near_ids[total] = near
        beside = lax.div(owner, 2) == chip
        far_ids[total] = jnp.where(beside, -1 - b, places[owner * blocks + b])

    total = jnp.int32(0)
    for s in range(1, shifts):
        ahead = lax.rem(me + s, n)
        behind = lax.rem(me + n - s, n)
        count = lists_ref[shifts + s, 0]

        @pl.loop(0, count)
        def _(t, total=total, ahead=ahead, s=s):
            add(total + t, lists_ref[s, 2 * t], ahead, lists_ref[s, 2 * t + 1])

        total = total + count
        count = all_lists_ref[behind * rows + shifts + s, 0]

        @pl.loop(0, count)
        def _(t, total=total, behind=behind, s=s):
            row = behind * rows + s
            add(total + t, all_lists_ref[row, 2 * t + 1], behind, all_lists_ref[row, 2 * t])

        total = total + count

    def fetch(t):
        place = far_ids[t]

        @pl.when(place < 0)
        def _():
            pltpu.make_async_copy(side_ref.at[-1 - place], held.at[lax.rem(t, 2)], sems.at[lax.rem(t, 2)]).start()

        @pl.when(place >= 0)
        def _():
            pltpu.make_async_copy(recv_ref.at[place], held.at[lax.rem(t, 2)], sems.at[lax.rem(t, 2)]).start()

    @pl.when(total > 0)
    def _():
        fetch(0)

    acc_ref[...] = acc_in[...]
    dens_ref[...] = dens_in[...]

    @pl.loop(0, total)
    def _(t):
        @pl.when(t + 1 < total)
        def _():
            fetch(t + 1)

        pltpu.make_async_copy(recv_ref.at[0], held.at[lax.rem(t, 2)], sems.at[lax.rem(t, 2)]).wait()
        a = near_ids[t]
        other = held[lax.rem(t, 2)]
        weights = kernel_of(unit_ref[a], other)
        dens_ref[a] += jnp.broadcast_to(jnp.sum(weights, axis=1, keepdims=True), (BLOCK, LANES))
        acc_ref[a] += jnp.dot(weights.astype(jnp.bfloat16), other, preferred_element_type=jnp.float32)

    @pl.loop(0, blocks)
    def _(i):
        dens = dens_ref[i]
        share = acc_ref[i] / dens[:, 0:1]
        out_ref[i] = (unit_ref[i].astype(jnp.float32) - share).astype(jnp.bfloat16)
        log_ref[i] = jnp.log(dens.T[0:1])


def shards(embeddings, home_pairs, home_count, surplus_pairs):
    n = lax.axis_size("owner")
    groups = lax.axis_size("group")
    width = embeddings.shape[1]
    blocks = embeddings.shape[0] // BLOCK
    shifts = home_pairs.shape[2]
    slots = home_pairs.shape[3]
    surplus = surplus_pairs.shape[2]
    lanes = 2 * slots
    rows = -(-(2 * shifts + 1) // 8) * 8
    chips = n // 2

    extra = surplus_pairs[0, 0].reshape(1, -1)
    lists = jnp.concatenate(
        [
            home_pairs[0, 0].reshape(shifts, lanes),
            jnp.broadcast_to(home_count[0, 0][:, None], (shifts, lanes)),
            jnp.pad(extra, ((0, rows - 2 * shifts - 1), (0, lanes - extra.shape[1]))),
        ],
        axis=0,
    )
    emb = embeddings.reshape(blocks, BLOCK, width)
    vmem = pl.BlockSpec(memory_space=VMEM)
    smem = pl.BlockSpec(memory_space=SMEM)
    anyw = pl.BlockSpec(memory_space=ANY)
    shape = jax.ShapeDtypeStruct
    dma = pltpu.SemaphoreType.DMA
    blocks_shape = (blocks, BLOCK, width)
    tile = (blocks, LANES)

    unit, side, need, peak, all_lists = pl.pallas_call(
        functools.partial(plan_kernel, n, groups, shifts),
        out_shape=(
            shape(blocks_shape, jnp.bfloat16),
            shape(blocks_shape, jnp.bfloat16),
            shape(tile, jnp.int32),
            shape(tile, jnp.int32),
            shape((n, rows, lanes), jnp.int32),
        ),
        in_specs=[vmem, vmem],
        out_specs=(vmem, vmem, vmem, vmem, anyw),
        scratch_shapes=[
            pltpu.VMEM(blocks_shape, jnp.bfloat16),
            pltpu.VMEM(tile, jnp.float32),
            pltpu.VMEM((n,) + tile, jnp.float32),
            pltpu.VMEM(tile, jnp.float32),
            pltpu.VMEM((groups,) + tile, jnp.float32),
            dma, dma, dma((n,)), dma((n,)), dma((n,)), dma((n,)), dma((groups,)), dma((groups,)),
        ],
        compiler_params=pltpu.CompilerParams(
            collective_id=0, has_side_effects=True, vmem_limit_bytes=VMEM_BYTES
        ),
    )(lists, emb)

    packed, mask = pl.pallas_call(
        functools.partial(pack_kernel, n, shifts, surplus),
        out_shape=(
            shape(blocks_shape, jnp.bfloat16),
            shape((blocks, 1, blocks * BLOCK), jnp.float32),
        ),
        in_specs=[smem, smem, smem, anyw, anyw],
        out_specs=(vmem, vmem),
        scratch_shapes=[dma((2, blocks))],
        compiler_params=pltpu.CompilerParams(vmem_limit_bytes=VMEM_BYTES),
    )(lists, need, peak, unit, side)

    def exchange(place, capacity):
        def run(packed, unit, mask):
            return pl.pallas_call(
                functools.partial(exchange_kernel, n, capacity),
                out_shape=(
                    shape((chips, 2 * blocks, BLOCK, width), jnp.bfloat16),
                    shape(blocks_shape, jnp.float32),
                    shape((blocks, BLOCK, LANES), jnp.float32),
                ),
                in_specs=[anyw, vmem, vmem],
                out_specs=(anyw, vmem, vmem),
                scratch_shapes=[dma((chips, capacity)) for _ in range(4)],
                compiler_params=pltpu.CompilerParams(
                    collective_id=1 + place, has_side_effects=True, vmem_limit_bytes=VMEM_BYTES
                ),
            )(packed, unit, mask)

        return run

    branches = [exchange(i, min(c, blocks)) for i, c in enumerate(CAPACITIES + (blocks,))]
    recv, acc, dens = lax.switch(capacity_index(peak[0, 0], blocks), branches, packed, unit, mask)

    entries = 2 * shifts * slots
    centered, log_density = pl.pallas_call(
        functools.partial(far_kernel, n, shifts, rows),
        out_shape=(
            shape(blocks_shape, jnp.bfloat16),
            shape((blocks, 1, BLOCK), jnp.float32),
        ),
        in_specs=[smem, smem, smem, vmem, vmem, vmem, anyw, anyw],
        out_specs=(vmem, vmem),
        scratch_shapes=[
            pltpu.VMEM(blocks_shape, jnp.float32),
            pltpu.VMEM((blocks, BLOCK, LANES), jnp.float32),
            pltpu.SMEM((entries,), jnp.int32),
            pltpu.SMEM((entries,), jnp.int32),
            pltpu.SMEM((n * blocks,), jnp.int32),
            pltpu.VMEM((2, BLOCK, width), jnp.bfloat16),
            dma((2,)),
        ],
        compiler_params=pltpu.CompilerParams(vmem_limit_bytes=VMEM_BYTES),
    )(
        lists, all_lists.reshape(n * rows, lanes), need, unit, acc, dens, side,
        recv.reshape(chips * 2 * blocks, BLOCK, width),
    )
    return (centered.reshape(-1, width), log_density.reshape(-1))


def solution(mesh):
    return jax.shard_map(
        shards,
        mesh=mesh,
        in_specs=(
            P(("group", "owner"), None),
            P("group", "owner", None, None, None),
            P("group", "owner", None),
            P("group", "owner", None, None),
        ),
        out_specs=(P(("group", "owner"), None), P(("group", "owner"))),
        check_vma=False,
    )
```

```python
import functools

import jax
import jax.numpy as jnp
from jax import lax
from jax.experimental import pallas as pl
from jax.experimental.pallas import tpu as pltpu
from jax.sharding import PartitionSpec as P

BLOCK = 128
LANES = 128
VMEM_BYTES = 56 * 1024 * 1024

sharpness = 4.0
epsilon = 1e-06

VMEM = pltpu.MemorySpace.VMEM
SMEM = pltpu.MemorySpace.SMEM
ANY = pl.ANY


def kernel_of(first, second):
    width = first.shape[-1]
    similarity = lax.dot_general(
        first, second, (((1,), (1,)), ((), ())), preferred_element_type=jnp.float32
    ) * (1.0 / width)
    return jnp.exp(sharpness * (similarity - 1.0))


CAPACITIES = (2, 3, 4, 5, 6, 7, 8, 10, 12)
HALF = 64
DEPTH = 6


def capacities(blocks):
    return tuple(min(capacity, 2 * blocks) for capacity in CAPACITIES) + (2 * blocks,)


def choose(peak, blocks):
    index = jnp.int32(0)
    capacity = jnp.int32(2 * blocks)
    for smaller in reversed(capacities(blocks)[:-1]):
        index = index + jnp.where(peak > smaller, 1, 0).astype(jnp.int32)
        capacity = jnp.where(peak <= smaller, smaller, capacity)
    return index, capacity


def normalize(source_ref, target_ref, i):
    wide = source_ref[i].astype(jnp.float32)
    inv = lax.rsqrt(jnp.mean(wide * wide, axis=-1, keepdims=True) + epsilon)
    target_ref[i] = (wide * inv).astype(jnp.bfloat16)


def plan_kernel(
    n, groups, shifts, pairs_ref, count_ref, pairs_hbm, count_hbm, emb_ref,
    unit_ref, side_ref, need_ref, peak_ref, all_pairs_ref, all_count_ref,
    emb_side, tile, tiles, peak_tile, peaks,
    side_send, side_recv, pairs_send, pairs_recv, count_send, count_recv, tile_send, tile_recv, peak_send, peak_recv,
):
    group = lax.axis_index("group")
    me = lax.axis_index("owner")
    blocks = unit_ref.shape[0]
    slots = pairs_ref.shape[2]
    sibling = me + 1 - 2 * lax.rem(me, 2)

    barrier = pltpu.get_barrier_semaphore()
    for d in range(1, n):
        pl.semaphore_signal(barrier, inc=1, device_id={"owner": lax.rem(me + d, n)})
    for d in range(1, groups):
        pl.semaphore_signal(barrier, inc=1, device_id={"group": lax.rem(group + d, groups)})

    slot = lax.broadcasted_iota(jnp.int32, (blocks, slots), 1)
    block = lax.broadcasted_iota(jnp.int32, (blocks, slots), 0)
    owner_lane = lax.broadcasted_iota(jnp.int32, (blocks, LANES), 1)
    need = jnp.zeros((blocks, LANES), jnp.float32)
    for s in range(1, shifts):
        partner = lax.rem(me + s, n)
        scale = jnp.where(lax.div(partner, 2) != lax.div(me, 2), 1.0, 0.0)
        listed = pairs_ref[s]
        for side, owner in enumerate((me, partner)):
            named = jnp.broadcast_to(listed[side : side + 1], (blocks, slots))
            hit = jnp.where((named == block) & (slot < count_ref[0, s]), 1.0, 0.0)
            column = jnp.max(hit, axis=1, keepdims=True)
            need = jnp.maximum(need, jnp.where(owner_lane == owner, column, 0.0) * scale)
    tile[...] = need

    @pl.loop(0, blocks)
    def _(i):
        normalize(emb_ref, unit_ref, i)

    pl.semaphore_wait(barrier, n + groups - 2)

    def to_owner(source, target, send, recv, d):
        return pltpu.make_async_remote_copy(
            src_ref=source, dst_ref=target.at[d], send_sem=send.at[d], recv_sem=recv.at[d],
            device_id={"owner": lax.rem(me + d, n)},
        )

    def list_copies(d):
        target = {"owner": lax.rem(me + d, n)}
        return (
            pltpu.make_async_remote_copy(
                src_ref=pairs_hbm, dst_ref=all_pairs_ref.at[me],
                send_sem=pairs_send.at[d], recv_sem=pairs_recv.at[d], device_id=target,
            ),
            pltpu.make_async_remote_copy(
                src_ref=count_hbm, dst_ref=all_count_ref.at[me],
                send_sem=count_send.at[d], recv_sem=count_recv.at[d], device_id=target,
            ),
        )

    def peak_copy(d):
        return pltpu.make_async_remote_copy(
            src_ref=peak_tile, dst_ref=peaks.at[d], send_sem=peak_send.at[d], recv_sem=peak_recv.at[d],
            device_id={"group": lax.rem(group + d, groups)},
        )

    for d in range(1, n):
        to_owner(tile, tiles, tile_send, tile_recv, d).start()
    side = pltpu.make_async_remote_copy(
        src_ref=emb_ref, dst_ref=emb_side, send_sem=side_send, recv_sem=side_recv,
        device_id={"owner": sibling},
    )
    side.start()
    for d in range(1, n):
        for copy in list_copies(d):
            copy.start()

    for d in range(1, n):
        to_owner(tile, tiles, tile_send, tile_recv, d).wait()
    need = tile[...]
    for d in range(1, n):
        need = jnp.maximum(need, tiles[d])
    need_ref[...] = need.astype(jnp.int32)
    peak = jnp.zeros((1, 1), jnp.float32)
    for chip in range(n // 2):
        on_chip = jnp.where(lax.div(owner_lane, 2) == chip, need, 0.0)
        total = jnp.sum(jnp.sum(on_chip, axis=1, keepdims=True), axis=0, keepdims=True)
        peak = jnp.maximum(peak, total)
    peak_tile[...] = jnp.broadcast_to(peak, peak_tile.shape)

    side.wait()
    early = 2

    @pl.loop(0, early)
    def _(i):
        normalize(emb_side, side_ref, i)

    for d in range(1, groups):
        peak_copy(d).start()

    @pl.loop(early, blocks)
    def _(i):
        normalize(emb_side, side_ref, i)

    for d in range(1, groups):
        peak_copy(d).wait()
    highest = peak_tile[...]
    for d in range(1, groups):
        highest = jnp.maximum(highest, peaks[d])
    peak_ref[...] = highest.astype(jnp.int32)
    for d in range(1, n):
        for copy in list_copies(d):
            copy.wait()


def pack_kernel(
    n, pairs_ref, count_ref, surplus_ref, need_ref, peak_ref, unit_ref, side_ref,
    packed_ref, mask_ref, index_ref, sems,
):
    me = lax.axis_index("owner")
    core = lax.rem(me, 2)
    halves = packed_ref.shape[0]
    blocks = halves // 2
    index, capacity = choose(peak_ref[0, 0], blocks)
    index_ref[0, 0] = index

    rank = jnp.int32(0)
    taken = []
    for half in range(2):
        owner = me - core + half
        for b in range(blocks):
            needed = need_ref[b, owner] == 1
            for part in range(2):
                slot = rank + part - core * capacity
                ours = needed & (slot >= 0) & (slot < capacity)
                place = jnp.clip(slot, 0, halves - 1)
                for own in (True, False):
                    source = unit_ref if own else side_ref
                    chosen = ours & ((core == half) == own)
                    copy = pltpu.make_async_copy(
                        source.at[2 * b + part], packed_ref.at[place], sems.at[half, 2 * b + part]
                    )

                    @pl.when(chosen)
                    def _(copy=copy):
                        copy.start()

                    taken.append((chosen, copy))
            rank = rank + 2 * needed.astype(jnp.int32)

    mask_ref[...] = jnp.zeros_like(mask_ref)
    one = jnp.ones((1, BLOCK), jnp.float32)

    def mark(a, b):
        mask_ref[a, :, pl.ds(pl.multiple_of(b * BLOCK, BLOCK), BLOCK)] = one
        mask_ref[b, :, pl.ds(pl.multiple_of(a * BLOCK, BLOCK), BLOCK)] = one

    @pl.loop(0, count_ref[0, 0])
    def _(t):
        mark(pairs_ref[0, 0, t], pairs_ref[0, 1, t])

    @pl.loop(0, surplus_ref.shape[1])
    def _(t):
        @pl.when(surplus_ref[2, t] == 1)
        def _():
            mark(surplus_ref[0, t], surplus_ref[1, t])

    for chosen, copy in taken:
        @pl.when(chosen)
        def _(copy=copy):
            copy.wait()


def exchange_kernel(
    n, capacity, packed_ref, unit_ref, mask_ref, recv_ref, acc_out, dens_out,
    acc_ref, dens_ref, out_sems, send_sem, recv_sem, fwd_send, fwd_recv,
):
    me = lax.axis_index("owner")
    blocks = unit_ref.shape[0]
    width = unit_ref.shape[2]
    chips = n // 2
    chip = lax.div(me, 2)
    core = lax.rem(me, 2)
    sibling = me + 1 - 2 * core

    barrier = pltpu.get_barrier_semaphore()
    pl.semaphore_signal(barrier, inc=1, device_id={"owner": sibling})
    for k in range(1, chips):
        pl.semaphore_signal(barrier, inc=1, device_id={"owner": lax.rem(me + 2 * k, n)})
    pl.semaphore_wait(barrier, chips)

    def cross_copy(k, i):
        return pltpu.make_async_remote_copy(
            src_ref=packed_ref.at[i], dst_ref=recv_ref.at[chip, core * capacity + i],
            send_sem=send_sem.at[k, i], recv_sem=recv_sem.at[k, i],
            device_id={"owner": lax.rem(me + 2 * k, n)},
        )

    def forward_copy(k, i):
        source = lax.rem(chip + chips - k, chips)
        landed = recv_ref.at[source, core * capacity + i]
        return pltpu.make_async_remote_copy(
            src_ref=landed, dst_ref=landed,
            send_sem=fwd_send.at[k, i], recv_sem=fwd_recv.at[k, i],
            device_id={"owner": sibling},
        )

    for i in range(capacity):
        for k in range(1, chips):
            cross_copy(k, i).start()

    every = unit_ref[...].reshape(blocks * BLOCK, width)

    @pl.loop(0, blocks // 2)
    def _(c):
        rows = unit_ref[pl.ds(2 * c, 2)].reshape(2 * BLOCK, width)
        upper = jnp.broadcast_to(mask_ref[2 * c], (BLOCK, blocks * BLOCK))
        lower = jnp.broadcast_to(mask_ref[2 * c + 1], (BLOCK, blocks * BLOCK))
        weights = kernel_of(rows, every) * jnp.concatenate([upper, lower], axis=0)
        total = jnp.sum(weights, axis=1, keepdims=True)
        dens_ref[pl.ds(2 * c, 2)] = jnp.broadcast_to(total, (2 * BLOCK, LANES)).reshape(2, BLOCK, LANES)
        near = jnp.dot(weights.astype(jnp.bfloat16), every, preferred_element_type=jnp.float32)
        acc_ref[pl.ds(2 * c, 2)] = near.reshape(2, BLOCK, width)

    results = (
        pltpu.make_async_copy(acc_ref, acc_out, out_sems.at[0]),
        pltpu.make_async_copy(dens_ref, dens_out, out_sems.at[1]),
    )
    for i in range(capacity):
        for k in range(1, chips):
            cross_copy(k, i).wait_recv()
            forward_copy(k, i).start()
        if i == 0:
            for copy in results:
                copy.start()
    for copy in results:
        copy.wait()
    for i in range(capacity):
        for k in range(1, chips):
            cross_copy(k, i).wait_send()
            forward_copy(k, i).wait()


def far_kernel(
    n, pairs_ref, count_ref, all_pairs_ref, all_count_ref, need_ref, unit_ref, acc_in, dens_in, side_ref, recv_ref,
    out_ref, log_ref, acc_ref, dens_ref, near_ids, far_ids, places, held, sems, in_sems,
):
    me = lax.axis_index("owner")
    blocks = unit_ref.shape[0]
    width = unit_ref.shape[2]
    chip = lax.div(me, 2)
    pool = 2 * blocks
    shifts = pairs_ref.shape[0]
    loads = (
        pltpu.make_async_copy(acc_in, acc_ref, in_sems.at[0]),
        pltpu.make_async_copy(dens_in, dens_ref, in_sems.at[1]),
    )
    for copy in loads:
        copy.start()

    for source in range(n // 2):
        rank = jnp.int32(0)
        for half in range(2):
            for b in range(blocks):
                owner = 2 * source + half
                places[owner * blocks + b] = source * pool + rank
                rank = rank + need_ref[b, owner]

    def add(total, near, owner, b):
        near_ids[total] = near
        beside = lax.div(owner, 2) == chip
        far_ids[total] = jnp.where(beside, -1 - b, places[owner * blocks + b])

    total = jnp.int32(0)
    for s in range(1, shifts):
        ahead = lax.rem(me + s, n)
        behind = lax.rem(me + n - s, n)
        count = count_ref[0, s]

        @pl.loop(0, count)
        def _(t, total=total, ahead=ahead, s=s):
            add(total + t, pairs_ref[s, 0, t], ahead, pairs_ref[s, 1, t])

        total = total + count
        count = all_count_ref[behind, 0, s]

        @pl.loop(0, count)
        def _(t, total=total, behind=behind, s=s):
            add(total + t, all_pairs_ref[behind, s, 1, t], behind, all_pairs_ref[behind, s, 0, t])

        total = total + count

    def fetch(t):
        place = far_ids[t]

        @pl.when(place < 0)
        def _():
            pltpu.make_async_copy(side_ref.at[-1 - place], held.at[lax.rem(t, DEPTH)], sems.at[lax.rem(t, DEPTH)]).start()

        @pl.when(place >= 0)
        def _():
            pltpu.make_async_copy(recv_ref.at[place], held.at[lax.rem(t, DEPTH)], sems.at[lax.rem(t, DEPTH)]).start()

    @pl.loop(0, jnp.minimum(total, DEPTH - 1))
    def _(t):
        fetch(t)

    for copy in loads:
        copy.wait()

    @pl.loop(0, total)
    def _(t):
        @pl.when(t + DEPTH - 1 < total)
        def _():
            fetch(t + DEPTH - 1)

        pltpu.make_async_copy(recv_ref.at[0], held.at[lax.rem(t, DEPTH)], sems.at[lax.rem(t, DEPTH)]).wait()
        a = near_ids[t]
        other = held[lax.rem(t, DEPTH)]
        weights = kernel_of(unit_ref[a], other)
        dens_ref[a] += jnp.broadcast_to(jnp.sum(weights, axis=1, keepdims=True), (BLOCK, LANES))
        acc_ref[a] += jnp.dot(weights.astype(jnp.bfloat16), other, preferred_element_type=jnp.float32)

    @pl.loop(0, blocks)
    def _(i):
        dens = dens_ref[i]
        share = acc_ref[i] * (1.0 / dens[:, 0:1])
        out_ref[i] = (unit_ref[i].astype(jnp.float32) - share).astype(jnp.bfloat16)
        log_ref[i] = jnp.log(dens.T[0:1])


def shards(embeddings, home_pairs, home_count, surplus_pairs):
    n = lax.axis_size("owner")
    groups = lax.axis_size("group")
    width = embeddings.shape[1]
    blocks = embeddings.shape[0] // BLOCK
    shifts = home_pairs.shape[2]
    slots = home_pairs.shape[3]
    chips = n // 2

    pairs = jnp.transpose(home_pairs[0, 0], (0, 2, 1))
    count = home_count[0]
    extra = jnp.transpose(surplus_pairs[0, 0], (1, 0))
    emb = embeddings.reshape(blocks, BLOCK, width)
    vmem = pl.BlockSpec(memory_space=VMEM)
    smem = pl.BlockSpec(memory_space=SMEM)
    anyw = pl.BlockSpec(memory_space=ANY)
    shape = jax.ShapeDtypeStruct
    dma = pltpu.SemaphoreType.DMA
    blocks_shape = (blocks, BLOCK, width)
    tile = (blocks, LANES)

    unit, side, need, peak, all_pairs, all_count = pl.pallas_call(
        functools.partial(plan_kernel, n, groups, shifts),
        out_shape=(
            shape(blocks_shape, jnp.bfloat16),
            shape(blocks_shape, jnp.bfloat16),
            shape(tile, jnp.int32),
            shape(tile, jnp.int32),
            shape((n,) + pairs.shape, jnp.int32),
            shape((n,) + count.shape, jnp.int32),
        ),
        in_specs=[vmem, smem, anyw, anyw, vmem],
        out_specs=(vmem, vmem, vmem, vmem, anyw, anyw),
        scratch_shapes=[
            pltpu.VMEM(blocks_shape, jnp.bfloat16),
            pltpu.VMEM(tile, jnp.float32),
            pltpu.VMEM((n,) + tile, jnp.float32),
            pltpu.VMEM(tile, jnp.float32),
            pltpu.VMEM((groups,) + tile, jnp.float32),
            dma, dma, dma((n,)), dma((n,)), dma((n,)), dma((n,)), dma((n,)), dma((n,)),
            dma((groups,)), dma((groups,)),
        ],
        compiler_params=pltpu.CompilerParams(
            collective_id=0, has_side_effects=True, vmem_limit_bytes=VMEM_BYTES
        ),
    )(pairs, count, pairs, count, emb)

    halved = (2 * blocks, HALF, width)
    packed, mask, index = pl.pallas_call(
        functools.partial(pack_kernel, n),
        out_shape=(
            shape(halved, jnp.bfloat16),
            shape((blocks, 1, blocks * BLOCK), jnp.float32),
            shape((1, 1), jnp.int32),
        ),
        in_specs=[smem, smem, smem, smem, smem, anyw, anyw],
        out_specs=(vmem, vmem, smem),
        scratch_shapes=[dma((2, 2 * blocks))],
        compiler_params=pltpu.CompilerParams(vmem_limit_bytes=VMEM_BYTES),
    )(pairs, count, extra, need, peak, unit.reshape(halved), side.reshape(halved))

    def exchange(place, capacity):
        def run(packed, unit, mask):
            return pl.pallas_call(
                functools.partial(exchange_kernel, n, capacity),
                out_shape=(
                    shape((chips, 4 * blocks, HALF, width), jnp.bfloat16),
                    shape(blocks_shape, jnp.float32),
                    shape((blocks, BLOCK, LANES), jnp.float32),
                ),
                in_specs=[anyw, vmem, vmem],
                out_specs=(anyw, anyw, anyw),
                scratch_shapes=[
                    pltpu.VMEM(blocks_shape, jnp.float32),
                    pltpu.VMEM((blocks, BLOCK, LANES), jnp.float32),
                    dma((2,)),
                ] + [dma((chips, capacity)) for _ in range(4)],
                compiler_params=pltpu.CompilerParams(
                    collective_id=1 + place, has_side_effects=True, vmem_limit_bytes=VMEM_BYTES
                ),
            )(packed, unit, mask)

        return run

    branches = [exchange(i, c) for i, c in enumerate(capacities(blocks))]
    recv, acc, dens = lax.switch(index.reshape(()), branches, packed, unit, mask)

    entries = 2 * shifts * slots
    centered, log_density = pl.pallas_call(
        functools.partial(far_kernel, n),
        out_shape=(
            shape(blocks_shape, jnp.bfloat16),
            shape((blocks, 1, BLOCK), jnp.float32),
        ),
        in_specs=[smem, smem, smem, smem, smem, vmem, anyw, anyw, anyw, anyw],
        out_specs=(vmem, vmem),
        scratch_shapes=[
            pltpu.VMEM(blocks_shape, jnp.float32),
            pltpu.VMEM((blocks, BLOCK, LANES), jnp.float32),
            pltpu.SMEM((entries,), jnp.int32),
            pltpu.SMEM((entries,), jnp.int32),
            pltpu.SMEM((n * blocks,), jnp.int32),
            pltpu.VMEM((DEPTH, BLOCK, width), jnp.bfloat16),
            dma((DEPTH,)),
            dma((2,)),
        ],
        compiler_params=pltpu.CompilerParams(vmem_limit_bytes=VMEM_BYTES),
    )(
        pairs, count, all_pairs, all_count, need, unit, acc, dens, side,
        recv.reshape(chips * 2 * blocks, BLOCK, width),
    )
    return (centered.reshape(-1, width), log_density.reshape(-1))


def solution(mesh):
    return jax.shard_map(
        shards,
        mesh=mesh,
        in_specs=(
            P(("group", "owner"), None),
            P("group", "owner", None, None, None),
            P("group", "owner", None),
            P("group", "owner", None, None),
        ),
        out_specs=(P(("group", "owner"), None), P(("group", "owner"))),
        check_vma=False,
    )
```

```python
import functools

import jax
import jax.numpy as jnp
from jax import lax
from jax.experimental import pallas as pl
from jax.experimental.pallas import tpu as pltpu
from jax.sharding import PartitionSpec as P

BLOCK = 128
LANES = 128
VMEM_BYTES = 56 * 1024 * 1024

sharpness = 4.0
epsilon = 1e-06

VMEM = pltpu.MemorySpace.VMEM
SMEM = pltpu.MemorySpace.SMEM
ANY = pl.ANY


def kernel_of(first, second):
    width = first.shape[-1]
    similarity = lax.dot_general(
        first, second, (((1,), (1,)), ((), ())), preferred_element_type=jnp.float32
    ) * (1.0 / width)
    return jnp.exp(sharpness * (similarity - 1.0))


CAPACITIES = (2, 3, 4, 5, 6, 7, 8, 10, 12)
HALF = 64
DEPTH = 6


def capacities(blocks):
    return tuple(min(capacity, 2 * blocks) for capacity in CAPACITIES) + (2 * blocks,)


def choose(peak, blocks):
    index = jnp.int32(0)
    capacity = jnp.int32(2 * blocks)
    for smaller in reversed(capacities(blocks)[:-1]):
        index = index + jnp.where(peak > smaller, 1, 0).astype(jnp.int32)
        capacity = jnp.where(peak <= smaller, smaller, capacity)
    return index, capacity


def normalize(source_ref, target_ref, i):
    wide = source_ref[i].astype(jnp.float32)
    inv = lax.rsqrt(jnp.mean(wide * wide, axis=-1, keepdims=True) + epsilon)
    target_ref[i] = (wide * inv).astype(jnp.bfloat16)


def plan_kernel(
    n, groups, shifts, pairs_ref, count_ref, surplus_ref, pairs_hbm, count_hbm, emb_ref,
    unit_ref, side_ref, need_ref, peak_ref, mask_ref, all_pairs_ref, all_count_ref,
    tile, tiles, peak_tile, peaks,
    side_send, side_recv, pairs_send, pairs_recv, count_send, count_recv, tile_send, tile_recv, peak_send, peak_recv,
):
    group = lax.axis_index("group")
    me = lax.axis_index("owner")
    blocks = unit_ref.shape[0]
    slots = pairs_ref.shape[2]
    sibling = me + 1 - 2 * lax.rem(me, 2)

    barrier = pltpu.get_barrier_semaphore()
    for d in range(1, n):
        pl.semaphore_signal(barrier, inc=1, device_id={"owner": lax.rem(me + d, n)})
    for d in range(1, groups):
        pl.semaphore_signal(barrier, inc=1, device_id={"group": lax.rem(group + d, groups)})

    slot = lax.broadcasted_iota(jnp.int32, (blocks, slots), 1)
    block = lax.broadcasted_iota(jnp.int32, (blocks, slots), 0)
    owner_lane = lax.broadcasted_iota(jnp.int32, (blocks, LANES), 1)
    need = jnp.zeros((blocks, LANES), jnp.float32)
    for s in range(1, shifts):
        partner = lax.rem(me + s, n)
        scale = jnp.where(lax.div(partner, 2) != lax.div(me, 2), 1.0, 0.0)
        listed = pairs_ref[s]
        for side, owner in enumerate((me, partner)):
            named = jnp.broadcast_to(listed[side : side + 1], (blocks, slots))
            hit = jnp.where((named == block) & (slot < count_ref[0, s]), 1.0, 0.0)
            column = jnp.max(hit, axis=1, keepdims=True)
            need = jnp.maximum(need, jnp.where(owner_lane == owner, column, 0.0) * scale)
    tile[...] = need

    @pl.loop(0, blocks)
    def _(i):
        normalize(emb_ref, unit_ref, i)

    pl.semaphore_wait(barrier, n + groups - 2)

    def to_owner(source, target, send, recv, d):
        return pltpu.make_async_remote_copy(
            src_ref=source, dst_ref=target.at[d], send_sem=send.at[d], recv_sem=recv.at[d],
            device_id={"owner": lax.rem(me + d, n)},
        )

    def list_copies(d):
        target = {"owner": lax.rem(me + d, n)}
        return (
            pltpu.make_async_remote_copy(
                src_ref=pairs_hbm, dst_ref=all_pairs_ref.at[me],
                send_sem=pairs_send.at[d], recv_sem=pairs_recv.at[d], device_id=target,
            ),
            pltpu.make_async_remote_copy(
                src_ref=count_hbm, dst_ref=all_count_ref.at[me],
                send_sem=count_send.at[d], recv_sem=count_recv.at[d], device_id=target,
            ),
        )

    def peak_copy(d):
        return pltpu.make_async_remote_copy(
            src_ref=peak_tile, dst_ref=peaks.at[d], send_sem=peak_send.at[d], recv_sem=peak_recv.at[d],
            device_id={"group": lax.rem(group + d, groups)},
        )

    for d in range(1, n):
        to_owner(tile, tiles, tile_send, tile_recv, d).start()

    def side_copy(i):
        return pltpu.make_async_remote_copy(
            src_ref=unit_ref.at[i], dst_ref=side_ref.at[i], send_sem=side_send.at[i], recv_sem=side_recv.at[i],
            device_id={"owner": sibling},
        )

    for d in range(1, n):
        for copy in list_copies(d):
            copy.start()
    for i in range(blocks):
        side_copy(i).start()

    def one_hot(ids, keep):
        shape = (blocks, ids.shape[1])
        index = lax.broadcasted_iota(jnp.int32, shape, 0)
        return jnp.where((jnp.broadcast_to(ids, shape) == index) & keep, 1.0, 0.0)

    def joined(first, second):
        along = (((1,), (1,)), ((), ()))
        forth = lax.dot_general(first, second, along, preferred_element_type=jnp.float32)
        return forth + lax.dot_general(second, first, along, preferred_element_type=jnp.float32)

    home = pairs_ref[0]
    listed = slot < count_ref[0, 0]
    marks = joined(one_hot(home[0:1], listed), one_hot(home[1:2], listed))
    live = jnp.broadcast_to(surplus_ref[0, 2], (blocks, surplus_ref.shape[3])) == 1
    marks = marks + joined(one_hot(surplus_ref[0, 0], live), one_hot(surplus_ref[0, 1], live))
    wide = (blocks, blocks * BLOCK)
    spread = lax.div(lax.broadcasted_iota(jnp.int32, wide, 1), BLOCK) == lax.broadcasted_iota(jnp.int32, wide, 0)
    spread = jnp.where(spread, 1.0, 0.0)
    marks = jnp.where(marks > 0.5, 1.0, 0.0)
    marks = jnp.dot(marks, spread, preferred_element_type=jnp.float32)
    for i in range(blocks):
        mask_ref[i] = marks[i : i + 1]

    for d in range(1, n):
        to_owner(tile, tiles, tile_send, tile_recv, d).wait()
    need = tile[...]
    for d in range(1, n):
        need = jnp.maximum(need, tiles[d])
    need_ref[...] = need.astype(jnp.int32)
    peak = jnp.zeros((1, 1), jnp.float32)
    for chip in range(n // 2):
        on_chip = jnp.where(lax.div(owner_lane, 2) == chip, need, 0.0)
        total = jnp.sum(jnp.sum(on_chip, axis=1, keepdims=True), axis=0, keepdims=True)
        peak = jnp.maximum(peak, total)
    peak_tile[...] = jnp.broadcast_to(peak, peak_tile.shape)

    for d in range(1, n):
        for copy in list_copies(d):
            copy.wait()
    for d in range(1, groups):
        peak_copy(d).start()
    for i in range(blocks):
        side_copy(i).wait()
    for d in range(1, groups):
        peak_copy(d).wait()
    highest = peak_tile[...]
    for d in range(1, groups):
        highest = jnp.maximum(highest, peaks[d])
    peak_ref[...] = highest.astype(jnp.int32)


def pack_kernel(need_ref, peak_ref, unit_ref, side_ref, packed_ref, index_ref, sems):
    me = lax.axis_index("owner")
    core = lax.rem(me, 2)
    halves = packed_ref.shape[0]
    blocks = halves // 2
    index, capacity = choose(peak_ref[0, 0], blocks)
    index_ref[0, 0] = index
    start = core * capacity

    def copy_of(source, row, place):
        return pltpu.make_async_copy(source.at[row], packed_ref.at[place], sems.at[place])

    rank = jnp.int32(0)
    for half in range(2):
        owner = me - core + half
        for b in range(blocks):
            needed = need_ref[b, owner]

            @pl.when(needed == 1)
            def _(rank=rank, half=half, b=b):
                for part in range(2):
                    place = rank + part - start
                    inside = (place >= 0) & (place < capacity)

                    @pl.when(inside & (core == half))
                    def _(place=place, part=part):
                        copy_of(unit_ref, 2 * b + part, place).start()

                    @pl.when(inside & (core != half))
                    def _(place=place, part=part):
                        copy_of(side_ref, 2 * b + part, place).start()

            rank = rank + 2 * needed

    @pl.loop(0, jnp.clip(rank - start, 0, capacity))
    def _(place):
        copy_of(unit_ref, 0, place).wait()


def exchange_kernel(
    n, capacity, packed_ref, unit_ref, mask_ref, recv_ref, acc_out, dens_out,
    acc_ref, dens_ref, out_sems, send_sem, recv_sem, fwd_send, fwd_recv,
):
    me = lax.axis_index("owner")
    blocks = unit_ref.shape[0]
    width = unit_ref.shape[2]
    chips = n // 2
    chip = lax.div(me, 2)
    core = lax.rem(me, 2)
    sibling = me + 1 - 2 * core

    barrier = pltpu.get_barrier_semaphore()
    pl.semaphore_signal(barrier, inc=1, device_id={"owner": sibling})
    for k in range(1, chips):
        pl.semaphore_signal(barrier, inc=1, device_id={"owner": lax.rem(me + 2 * k, n)})
    pl.semaphore_wait(barrier, chips)

    def cross_copy(k, i):
        return pltpu.make_async_remote_copy(
            src_ref=packed_ref.at[i], dst_ref=recv_ref.at[chip, core * capacity + i],
            send_sem=send_sem.at[k, i], recv_sem=recv_sem.at[k, i],
            device_id={"owner": lax.rem(me + 2 * k, n)},
        )

    def forward_copy(k, i):
        source = lax.rem(chip + chips - k, chips)
        landed = recv_ref.at[source, core * capacity + i]
        return pltpu.make_async_remote_copy(
            src_ref=landed, dst_ref=landed,
            send_sem=fwd_send.at[k, i], recv_sem=fwd_recv.at[k, i],
            device_id={"owner": sibling},
        )

    for i in range(capacity):
        for k in range(1, chips):
            cross_copy(k, i).start()

    every = unit_ref[...].reshape(blocks * BLOCK, width)

    @pl.loop(0, blocks // 2)
    def _(c):
        rows = unit_ref[pl.ds(2 * c, 2)].reshape(2 * BLOCK, width)
        upper = jnp.broadcast_to(mask_ref[2 * c], (BLOCK, blocks * BLOCK))
        lower = jnp.broadcast_to(mask_ref[2 * c + 1], (BLOCK, blocks * BLOCK))
        weights = kernel_of(rows, every) * jnp.concatenate([upper, lower], axis=0)
        total = jnp.sum(weights, axis=1, keepdims=True)
        dens_ref[pl.ds(2 * c, 2)] = jnp.broadcast_to(total, (2 * BLOCK, LANES)).reshape(2, BLOCK, LANES)
        near = jnp.dot(weights.astype(jnp.bfloat16), every, preferred_element_type=jnp.float32)
        acc_ref[pl.ds(2 * c, 2)] = near.reshape(2, BLOCK, width)

    results = (
        pltpu.make_async_copy(acc_ref, acc_out, out_sems.at[0]),
        pltpu.make_async_copy(dens_ref, dens_out, out_sems.at[1]),
    )
    for i in range(capacity):
        for k in range(1, chips):
            cross_copy(k, i).wait_recv()
            forward_copy(k, i).start()
        if i == 0:
            for copy in results:
                copy.start()
    for copy in results:
        copy.wait()
    for i in range(capacity):
        for k in range(1, chips):
            cross_copy(k, i).wait_send()
            forward_copy(k, i).wait()


def far_kernel(
    n, pairs_ref, count_ref, all_pairs_ref, all_count_ref, need_ref, unit_ref, acc_in, dens_in, side_ref, recv_ref,
    out_ref, log_ref, acc_ref, dens_ref, near_ids, far_ids, places, held, sems, in_sems,
):
    me = lax.axis_index("owner")
    blocks = unit_ref.shape[0]
    width = unit_ref.shape[2]
    chip = lax.div(me, 2)
    pool = 2 * blocks
    shifts = pairs_ref.shape[0]
    loads = (
        pltpu.make_async_copy(acc_in, acc_ref, in_sems.at[0]),
        pltpu.make_async_copy(dens_in, dens_ref, in_sems.at[1]),
    )
    for copy in loads:
        copy.start()

    for source in range(n // 2):
        rank = jnp.int32(0)
        for half in range(2):
            for b in range(blocks):
                owner = 2 * source + half
                places[owner * blocks + b] = source * pool + rank
                rank = rank + need_ref[b, owner]

    def add(total, near, owner, b):
        near_ids[total] = near
        beside = lax.div(owner, 2) == chip
        far_ids[total] = jnp.where(beside, -1 - b, places[owner * blocks + b])

    total = jnp.int32(0)
    for s in range(1, shifts):
        ahead = lax.rem(me + s, n)
        behind = lax.rem(me + n - s, n)
        count = count_ref[0, s]

        @pl.loop(0, count)
        def _(t, total=total, ahead=ahead, s=s):
            add(total + t, pairs_ref[s, 0, t], ahead, pairs_ref[s, 1, t])

        total = total + count
        count = all_count_ref[behind, 0, s]

        @pl.loop(0, count)
        def _(t, total=total, behind=behind, s=s):
            add(total + t, all_pairs_ref[behind, s, 1, t], behind, all_pairs_ref[behind, s, 0, t])

        total = total + count

    def fetch(t):
        place = far_ids[t]

        @pl.when(place < 0)
        def _():
            pltpu.make_async_copy(side_ref.at[-1 - place], held.at[lax.rem(t, DEPTH)], sems.at[lax.rem(t, DEPTH)]).start()

        @pl.when(place >= 0)
        def _():
            pltpu.make_async_copy(recv_ref.at[place], held.at[lax.rem(t, DEPTH)], sems.at[lax.rem(t, DEPTH)]).start()

    @pl.loop(0, jnp.minimum(total, DEPTH - 1))
    def _(t):
        fetch(t)

    for copy in loads:
        copy.wait()

    @pl.loop(0, total)
    def _(t):
        @pl.when(t + DEPTH - 1 < total)
        def _():
            fetch(t + DEPTH - 1)

        pltpu.make_async_copy(recv_ref.at[0], held.at[lax.rem(t, DEPTH)], sems.at[lax.rem(t, DEPTH)]).wait()
        a = near_ids[t]
        other = held[lax.rem(t, DEPTH)]
        weights = kernel_of(unit_ref[a], other)
        dens_ref[a] += jnp.broadcast_to(jnp.sum(weights, axis=1, keepdims=True), (BLOCK, LANES))
        acc_ref[a] += jnp.dot(weights.astype(jnp.bfloat16), other, preferred_element_type=jnp.float32)

    @pl.loop(0, blocks)
    def _(i):
        dens = dens_ref[i]
        share = acc_ref[i] * (1.0 / dens[:, 0:1])
        out_ref[i] = (unit_ref[i].astype(jnp.float32) - share).astype(jnp.bfloat16)
        log_ref[i] = jnp.log(dens.T[0:1])


def shards(embeddings, home_pairs, home_count, surplus_pairs):
    n = lax.axis_size("owner")
    groups = lax.axis_size("group")
    width = embeddings.shape[1]
    blocks = embeddings.shape[0] // BLOCK
    shifts = home_pairs.shape[2]
    slots = home_pairs.shape[3]
    chips = n // 2

    pairs = jnp.transpose(home_pairs[0, 0], (0, 2, 1))
    count = home_count[0]
    extra = jnp.transpose(surplus_pairs, (0, 3, 1, 2))
    emb = embeddings.reshape(blocks, BLOCK, width)
    vmem = pl.BlockSpec(memory_space=VMEM)
    smem = pl.BlockSpec(memory_space=SMEM)
    anyw = pl.BlockSpec(memory_space=ANY)
    shape = jax.ShapeDtypeStruct
    dma = pltpu.SemaphoreType.DMA
    blocks_shape = (blocks, BLOCK, width)
    tile = (blocks, LANES)

    unit, side, need, peak, mask, all_pairs, all_count = pl.pallas_call(
        functools.partial(plan_kernel, n, groups, shifts),
        out_shape=(
            shape(blocks_shape, jnp.bfloat16),
            shape(blocks_shape, jnp.bfloat16),
            shape(tile, jnp.int32),
            shape(tile, jnp.int32),
            shape((blocks, 1, blocks * BLOCK), jnp.float32),
            shape((n,) + pairs.shape, jnp.int32),
            shape((n,) + count.shape, jnp.int32),
        ),
        in_specs=[vmem, smem, vmem, anyw, anyw, vmem],
        out_specs=(vmem, anyw, vmem, vmem, vmem, anyw, anyw),
        scratch_shapes=[
            pltpu.VMEM(tile, jnp.float32),
            pltpu.VMEM((n,) + tile, jnp.float32),
            pltpu.VMEM(tile, jnp.float32),
            pltpu.VMEM((groups,) + tile, jnp.float32),
            dma((blocks,)), dma((blocks,)), dma((n,)), dma((n,)), dma((n,)), dma((n,)), dma((n,)), dma((n,)),
            dma((groups,)), dma((groups,)),
        ],
        compiler_params=pltpu.CompilerParams(
            collective_id=0, has_side_effects=True, vmem_limit_bytes=VMEM_BYTES
        ),
    )(pairs, count, extra, pairs, count, emb)

    halved = (2 * blocks, HALF, width)
    packed, index = pl.pallas_call(
        pack_kernel,
        out_shape=(
            shape(halved, jnp.bfloat16),
            shape((1, 1), jnp.int32),
        ),
        in_specs=[smem, smem, anyw, anyw],
        out_specs=(vmem, smem),
        scratch_shapes=[dma((2 * blocks,))],
        compiler_params=pltpu.CompilerParams(vmem_limit_bytes=VMEM_BYTES),
    )(need, peak, unit.reshape(halved), side.reshape(halved))

    def exchange(place, capacity):
        def run(packed, unit, mask):
            return pl.pallas_call(
                functools.partial(exchange_kernel, n, capacity),
                out_shape=(
                    shape((chips, 4 * blocks, HALF, width), jnp.bfloat16),
                    shape(blocks_shape, jnp.float32),
                    shape((blocks, BLOCK, LANES), jnp.float32),
                ),
                in_specs=[anyw, vmem, vmem],
                out_specs=(anyw, anyw, anyw),
                scratch_shapes=[
                    pltpu.VMEM(blocks_shape, jnp.float32),
                    pltpu.VMEM((blocks, BLOCK, LANES), jnp.float32),
                    dma((2,)),
                ] + [dma((chips, capacity)) for _ in range(4)],
                compiler_params=pltpu.CompilerParams(
                    collective_id=1 + place, has_side_effects=True, vmem_limit_bytes=VMEM_BYTES
                ),
            )(packed, unit, mask)

        return run

    branches = [exchange(i, c) for i, c in enumerate(capacities(blocks))]
    recv, acc, dens = lax.switch(index.reshape(()), branches, packed, unit, mask)

    entries = 2 * shifts * slots
    centered, log_density = pl.pallas_call(
        functools.partial(far_kernel, n),
        out_shape=(
            shape(blocks_shape, jnp.bfloat16),
            shape((blocks, 1, BLOCK), jnp.float32),
        ),
        in_specs=[smem, smem, smem, smem, smem, vmem, anyw, anyw, anyw, anyw],
        out_specs=(vmem, vmem),
        scratch_shapes=[
            pltpu.VMEM(blocks_shape, jnp.float32),
            pltpu.VMEM((blocks, BLOCK, LANES), jnp.float32),
            pltpu.SMEM((entries,), jnp.int32),
            pltpu.SMEM((entries,), jnp.int32),
            pltpu.SMEM((n * blocks,), jnp.int32),
            pltpu.VMEM((DEPTH, BLOCK, width), jnp.bfloat16),
            dma((DEPTH,)),
            dma((2,)),
        ],
        compiler_params=pltpu.CompilerParams(vmem_limit_bytes=VMEM_BYTES),
    )(
        pairs, count, all_pairs, all_count, need, unit, acc, dens, side,
        recv.reshape(chips * 2 * blocks, BLOCK, width),
    )
    return (centered.reshape(-1, width), log_density.reshape(-1))


def solution(mesh):
    return jax.shard_map(
        shards,
        mesh=mesh,
        in_specs=(
            P(("group", "owner"), None),
            P("group", "owner", None, None, None),
            P("group", "owner", None),
            P("group", "owner", None, None),
        ),
        out_specs=(P(("group", "owner"), None), P(("group", "owner"))),
        check_vma=False,
    )
```

```python
import functools

import jax
import jax.numpy as jnp
from jax import lax
from jax.experimental import pallas as pl
from jax.experimental.pallas import tpu as pltpu
from jax.sharding import PartitionSpec as P

BLOCK = 128
LANES = 128
VMEM_BYTES = 56 * 1024 * 1024

sharpness = 4.0
epsilon = 1e-06

VMEM = pltpu.MemorySpace.VMEM
SMEM = pltpu.MemorySpace.SMEM
ANY = pl.ANY


def kernel_of(first, second):
    width = first.shape[-1]
    similarity = lax.dot_general(
        first, second, (((1,), (1,)), ((), ())), preferred_element_type=jnp.float32
    ) * (1.0 / width)
    return jnp.exp(sharpness * (similarity - 1.0))


CAPACITIES = (2, 3, 4, 5, 6, 7, 8, 10, 12)
HALF = 64
DEPTH = 6


def capacities(blocks):
    return tuple(min(capacity, 2 * blocks) for capacity in CAPACITIES) + (2 * blocks,)


def choose(peak, blocks):
    index = jnp.int32(0)
    capacity = jnp.int32(2 * blocks)
    for smaller in reversed(capacities(blocks)[:-1]):
        index = index + jnp.where(peak > smaller, 1, 0).astype(jnp.int32)
        capacity = jnp.where(peak <= smaller, smaller, capacity)
    return index, capacity


def normalize(source_ref, target_ref, i):
    wide = source_ref[i].astype(jnp.float32)
    inv = lax.rsqrt(jnp.mean(wide * wide, axis=-1, keepdims=True) + epsilon)
    target_ref[i] = (wide * inv).astype(jnp.bfloat16)


def plan_kernel(
    n, groups, shifts, pairs_ref, count_ref, surplus_ref, pairs_hbm, count_hbm, emb_hbm,
    unit_ref, side_ref, need_ref, peak_ref, mask_ref, all_pairs_ref, all_count_ref,
    emb_ref, emb_sems, tile, tiles, peak_tile, peaks,
    side_send, side_recv, pairs_send, pairs_recv, count_send, count_recv, tile_send, tile_recv, peak_send, peak_recv,
):
    group = lax.axis_index("group")
    me = lax.axis_index("owner")
    blocks = unit_ref.shape[0]
    slots = pairs_ref.shape[2]
    sibling = me + 1 - 2 * lax.rem(me, 2)

    barrier = pltpu.get_barrier_semaphore()
    for d in range(1, n):
        pl.semaphore_signal(barrier, inc=1, device_id={"owner": lax.rem(me + d, n)})
    for d in range(1, groups):
        pl.semaphore_signal(barrier, inc=1, device_id={"group": lax.rem(group + d, groups)})

    def load(i):
        return pltpu.make_async_copy(emb_hbm.at[i], emb_ref.at[i], emb_sems.at[i])

    for i in range(blocks):
        load(i).start()

    slot = lax.broadcasted_iota(jnp.int32, (blocks, slots), 1)
    block = lax.broadcasted_iota(jnp.int32, (blocks, slots), 0)
    owner_lane = lax.broadcasted_iota(jnp.int32, (blocks, LANES), 1)
    need = jnp.zeros((blocks, LANES), jnp.float32)
    for s in range(1, shifts):
        partner = lax.rem(me + s, n)
        scale = jnp.where(lax.div(partner, 2) != lax.div(me, 2), 1.0, 0.0)
        listed = pairs_ref[s]
        for side, owner in enumerate((me, partner)):
            named = jnp.broadcast_to(listed[side : side + 1], (blocks, slots))
            hit = jnp.where((named == block) & (slot < count_ref[0, s]), 1.0, 0.0)
            column = jnp.max(hit, axis=1, keepdims=True)
            need = jnp.maximum(need, jnp.where(owner_lane == owner, column, 0.0) * scale)
    tile[...] = need

    @pl.loop(0, blocks)
    def _(i):
        load(i).wait()
        normalize(emb_ref, unit_ref, i)

    pl.semaphore_wait(barrier, n + groups - 2)

    def to_owner(source, target, send, recv, d):
        return pltpu.make_async_remote_copy(
            src_ref=source, dst_ref=target.at[d], send_sem=send.at[d], recv_sem=recv.at[d],
            device_id={"owner": lax.rem(me + d, n)},
        )

    def list_copies(d):
        target = {"owner": lax.rem(me + d, n)}
        return (
            pltpu.make_async_remote_copy(
                src_ref=pairs_hbm, dst_ref=all_pairs_ref.at[me],
                send_sem=pairs_send.at[d], recv_sem=pairs_recv.at[d], device_id=target,
            ),
            pltpu.make_async_remote_copy(
                src_ref=count_hbm, dst_ref=all_count_ref.at[me],
                send_sem=count_send.at[d], recv_sem=count_recv.at[d], device_id=target,
            ),
        )

    def peak_copy(d):
        return pltpu.make_async_remote_copy(
            src_ref=peak_tile, dst_ref=peaks.at[d], send_sem=peak_send.at[d], recv_sem=peak_recv.at[d],
            device_id={"group": lax.rem(group + d, groups)},
        )

    for d in range(1, n):
        to_owner(tile, tiles, tile_send, tile_recv, d).start()

    def side_copy(i):
        return pltpu.make_async_remote_copy(
            src_ref=unit_ref.at[i], dst_ref=side_ref.at[i], send_sem=side_send.at[i], recv_sem=side_recv.at[i],
            device_id={"owner": sibling},
        )

    for d in range(1, n):
        for copy in list_copies(d):
            copy.start()
    for i in range(blocks):
        side_copy(i).start()

    def one_hot(ids, keep):
        shape = (blocks, ids.shape[1])
        index = lax.broadcasted_iota(jnp.int32, shape, 0)
        return jnp.where((jnp.broadcast_to(ids, shape) == index) & keep, 1.0, 0.0)

    def joined(first, second):
        along = (((1,), (1,)), ((), ()))
        forth = lax.dot_general(first, second, along, preferred_element_type=jnp.float32)
        return forth + lax.dot_general(second, first, along, preferred_element_type=jnp.float32)

    home = pairs_ref[0]
    listed = slot < count_ref[0, 0]
    marks = joined(one_hot(home[0:1], listed), one_hot(home[1:2], listed))
    live = jnp.broadcast_to(surplus_ref[0, 2], (blocks, surplus_ref.shape[3])) == 1
    marks = marks + joined(one_hot(surplus_ref[0, 0], live), one_hot(surplus_ref[0, 1], live))
    wide = (blocks, blocks * BLOCK)
    spread = lax.div(lax.broadcasted_iota(jnp.int32, wide, 1), BLOCK) == lax.broadcasted_iota(jnp.int32, wide, 0)
    spread = jnp.where(spread, 1.0, 0.0)
    marks = jnp.where(marks > 0.5, 1.0, 0.0)
    marks = jnp.dot(marks, spread, preferred_element_type=jnp.float32)
    for i in range(blocks):
        mask_ref[i] = marks[i : i + 1]

    for d in range(1, n):
        to_owner(tile, tiles, tile_send, tile_recv, d).wait()
    need = tile[...]
    for d in range(1, n):
        need = jnp.maximum(need, tiles[d])
    need_ref[...] = need.astype(jnp.int32)
    peak = jnp.zeros((1, 1), jnp.float32)
    for chip in range(n // 2):
        on_chip = jnp.where(lax.div(owner_lane, 2) == chip, need, 0.0)
        total = jnp.sum(jnp.sum(on_chip, axis=1, keepdims=True), axis=0, keepdims=True)
        peak = jnp.maximum(peak, total)
    peak_tile[...] = jnp.broadcast_to(peak, peak_tile.shape)

    for d in range(1, n):
        for copy in list_copies(d):
            copy.wait()
    for d in range(1, groups):
        peak_copy(d).start()
    for i in range(blocks):
        side_copy(i).wait()
    for d in range(1, groups):
        peak_copy(d).wait()
    highest = peak_tile[...]
    for d in range(1, groups):
        highest = jnp.maximum(highest, peaks[d])
    peak_ref[...] = highest.astype(jnp.int32)


def pack_kernel(need_ref, peak_ref, unit_ref, side_ref, packed_ref, index_ref, sems):
    me = lax.axis_index("owner")
    core = lax.rem(me, 2)
    halves = packed_ref.shape[0]
    blocks = halves // 2
    index, capacity = choose(peak_ref[0, 0], blocks)
    index_ref[0, 0] = index
    start = core * capacity

    def copy_of(source, row, place):
        return pltpu.make_async_copy(source.at[row], packed_ref.at[place], sems.at[place])

    rank = jnp.int32(0)
    for half in range(2):
        owner = me - core + half
        for b in range(blocks):
            needed = need_ref[b, owner]

            @pl.when(needed == 1)
            def _(rank=rank, half=half, b=b):
                for part in range(2):
                    place = rank + part - start
                    inside = (place >= 0) & (place < capacity)

                    @pl.when(inside & (core == half))
                    def _(place=place, part=part):
                        copy_of(unit_ref, 2 * b + part, place).start()

                    @pl.when(inside & (core != half))
                    def _(place=place, part=part):
                        copy_of(side_ref, 2 * b + part, place).start()

            rank = rank + 2 * needed

    @pl.loop(0, jnp.clip(rank - start, 0, capacity))
    def _(place):
        copy_of(unit_ref, 0, place).wait()


def exchange_kernel(
    n, capacity, packed_ref, unit_ref, mask_ref, recv_ref, acc_out, dens_out,
    acc_ref, dens_ref, out_sems, send_sem, recv_sem, fwd_send, fwd_recv,
):
    me = lax.axis_index("owner")
    blocks = unit_ref.shape[0]
    width = unit_ref.shape[2]
    chips = n // 2
    chip = lax.div(me, 2)
    core = lax.rem(me, 2)
    sibling = me + 1 - 2 * core

    barrier = pltpu.get_barrier_semaphore()
    pl.semaphore_signal(barrier, inc=1, device_id={"owner": sibling})
    for k in range(1, chips):
        pl.semaphore_signal(barrier, inc=1, device_id={"owner": lax.rem(me + 2 * k, n)})
    pl.semaphore_wait(barrier, chips)

    def cross_copy(k, i):
        return pltpu.make_async_remote_copy(
            src_ref=packed_ref.at[i], dst_ref=recv_ref.at[chip, core * capacity + i],
            send_sem=send_sem.at[k, i], recv_sem=recv_sem.at[k, i],
            device_id={"owner": lax.rem(me + 2 * k, n)},
        )

    def forward_copy(k, i):
        source = lax.rem(chip + chips - k, chips)
        landed = recv_ref.at[source, core * capacity + i]
        return pltpu.make_async_remote_copy(
            src_ref=landed, dst_ref=landed,
            send_sem=fwd_send.at[k, i], recv_sem=fwd_recv.at[k, i],
            device_id={"owner": sibling},
        )

    for i in range(capacity):
        for k in range(1, chips):
            cross_copy(k, i).start()

    every = unit_ref[...].reshape(blocks * BLOCK, width)

    @pl.loop(0, blocks // 2)
    def _(c):
        rows = unit_ref[pl.ds(2 * c, 2)].reshape(2 * BLOCK, width)
        upper = jnp.broadcast_to(mask_ref[2 * c], (BLOCK, blocks * BLOCK))
        lower = jnp.broadcast_to(mask_ref[2 * c + 1], (BLOCK, blocks * BLOCK))
        weights = kernel_of(rows, every) * jnp.concatenate([upper, lower], axis=0)
        total = jnp.sum(weights, axis=1, keepdims=True)
        dens_ref[pl.ds(2 * c, 2)] = jnp.broadcast_to(total, (2 * BLOCK, LANES)).reshape(2, BLOCK, LANES)
        near = jnp.dot(weights.astype(jnp.bfloat16), every, preferred_element_type=jnp.float32)
        acc_ref[pl.ds(2 * c, 2)] = near.reshape(2, BLOCK, width)

    results = (
        pltpu.make_async_copy(acc_ref, acc_out, out_sems.at[0]),
        pltpu.make_async_copy(dens_ref, dens_out, out_sems.at[1]),
    )
    for i in range(capacity):
        for k in range(1, chips):
            cross_copy(k, i).wait_recv()
            forward_copy(k, i).start()
        if i == 0:
            for copy in results:
                copy.start()
    for copy in results:
        copy.wait()
    for i in range(capacity):
        for k in range(1, chips):
            cross_copy(k, i).wait_send()
            forward_copy(k, i).wait()


def far_kernel(
    n, pairs_ref, count_ref, all_pairs_ref, all_count_ref, need_ref, unit_ref, acc_in, dens_in, side_ref, recv_ref,
    out_hbm, log_ref, out_ref, out_sems, acc_ref, dens_ref, near_ids, far_ids, places, held, sems, in_sems,
):
    me = lax.axis_index("owner")
    blocks = unit_ref.shape[0]
    width = unit_ref.shape[2]
    chip = lax.div(me, 2)
    pool = 2 * blocks
    shifts = pairs_ref.shape[0]
    loads = (
        pltpu.make_async_copy(acc_in, acc_ref, in_sems.at[0]),
        pltpu.make_async_copy(dens_in, dens_ref, in_sems.at[1]),
    )
    for copy in loads:
        copy.start()

    for source in range(n // 2):
        rank = jnp.int32(0)
        for half in range(2):
            for b in range(blocks):
                owner = 2 * source + half
                places[owner * blocks + b] = source * pool + rank
                rank = rank + need_ref[b, owner]

    def add(total, near, owner, b):
        near_ids[total] = near
        beside = lax.div(owner, 2) == chip
        far_ids[total] = jnp.where(beside, -1 - b, places[owner * blocks + b])

    total = jnp.int32(0)
    for s in range(1, shifts):
        ahead = lax.rem(me + s, n)
        behind = lax.rem(me + n - s, n)
        count = count_ref[0, s]

        @pl.loop(0, count)
        def _(t, total=total, ahead=ahead, s=s):
            add(total + t, pairs_ref[s, 0, t], ahead, pairs_ref[s, 1, t])

        total = total + count
        count = all_count_ref[behind, 0, s]

        @pl.loop(0, count)
        def _(t, total=total, behind=behind, s=s):
            add(total + t, all_pairs_ref[behind, s, 1, t], behind, all_pairs_ref[behind, s, 0, t])

        total = total + count

    def fetch(t):
        place = far_ids[t]

        @pl.when(place < 0)
        def _():
            pltpu.make_async_copy(side_ref.at[-1 - place], held.at[lax.rem(t, DEPTH)], sems.at[lax.rem(t, DEPTH)]).start()

        @pl.when(place >= 0)
        def _():
            pltpu.make_async_copy(recv_ref.at[place], held.at[lax.rem(t, DEPTH)], sems.at[lax.rem(t, DEPTH)]).start()

    padded = 2 * lax.div(total + 1, 2)

    @pl.when(padded > total)
    def _():
        near_ids[total] = near_ids[total - 1]
        far_ids[total] = far_ids[total - 1]

    @pl.loop(0, jnp.minimum(padded, DEPTH - 2))
    def _(t):
        fetch(t)

    for copy in loads:
        copy.wait()

    @pl.loop(0, lax.div(padded, 2))
    def _(step):
        first = 2 * step

        @pl.when(first + DEPTH - 2 < padded)
        def _():
            fetch(first + DEPTH - 2)
            fetch(first + DEPTH - 1)

        for part in range(2):
            held_slot = lax.rem(first + part, DEPTH)
            pltpu.make_async_copy(recv_ref.at[0], held.at[held_slot], sems.at[held_slot]).wait()
        results = []
        for part in range(2):
            t = first + part
            a = near_ids[t]
            other = held[lax.rem(t, DEPTH)]
            weights = kernel_of(unit_ref[a], other)
            if part == 1:
                weights = jnp.where(t < total, weights, 0.0)
            results.append((a, weights, jnp.dot(weights.astype(jnp.bfloat16), other, preferred_element_type=jnp.float32)))
        for a, weights, sums in results:
            dens_ref[a] += jnp.broadcast_to(jnp.sum(weights, axis=1, keepdims=True), (BLOCK, LANES))
            acc_ref[a] += sums

    def put(i):
        return pltpu.make_async_copy(out_ref.at[i], out_hbm.at[i], out_sems.at[i])

    @pl.loop(0, blocks)
    def _(i):
        dens = dens_ref[i]
        share = acc_ref[i] * (1.0 / dens[:, 0:1])
        out_ref[i] = (unit_ref[i].astype(jnp.float32) - share).astype(jnp.bfloat16)
        log_ref[i] = jnp.log(dens.T[0:1])

        @pl.when(i > 0)
        def _():
            put(i - 1).start()

    put(blocks - 1).start()
    for i in range(blocks):
        put(i).wait()


def shards(embeddings, home_pairs, home_count, surplus_pairs):
    n = lax.axis_size("owner")
    groups = lax.axis_size("group")
    width = embeddings.shape[1]
    blocks = embeddings.shape[0] // BLOCK
    shifts = home_pairs.shape[2]
    slots = home_pairs.shape[3]
    chips = n // 2

    pairs = jnp.transpose(home_pairs[0, 0], (0, 2, 1))
    count = home_count[0]
    extra = jnp.transpose(surplus_pairs, (0, 3, 1, 2))
    emb = embeddings.reshape(blocks, BLOCK, width)
    vmem = pl.BlockSpec(memory_space=VMEM)
    smem = pl.BlockSpec(memory_space=SMEM)
    anyw = pl.BlockSpec(memory_space=ANY)
    shape = jax.ShapeDtypeStruct
    dma = pltpu.SemaphoreType.DMA
    blocks_shape = (blocks, BLOCK, width)
    tile = (blocks, LANES)

    unit, side, need, peak, mask, all_pairs, all_count = pl.pallas_call(
        functools.partial(plan_kernel, n, groups, shifts),
        out_shape=(
            shape(blocks_shape, jnp.bfloat16),
            shape(blocks_shape, jnp.bfloat16),
            shape(tile, jnp.int32),
            shape(tile, jnp.int32),
            shape((blocks, 1, blocks * BLOCK), jnp.float32),
            shape((n,) + pairs.shape, jnp.int32),
            shape((n,) + count.shape, jnp.int32),
        ),
        in_specs=[vmem, smem, vmem, anyw, anyw, anyw],
        out_specs=(vmem, anyw, vmem, vmem, vmem, anyw, anyw),
        scratch_shapes=[
            pltpu.VMEM(blocks_shape, jnp.bfloat16),
            dma((blocks,)),
            pltpu.VMEM(tile, jnp.float32),
            pltpu.VMEM((n,) + tile, jnp.float32),
            pltpu.VMEM(tile, jnp.float32),
            pltpu.VMEM((groups,) + tile, jnp.float32),
            dma((blocks,)), dma((blocks,)), dma((n,)), dma((n,)), dma((n,)), dma((n,)), dma((n,)), dma((n,)),
            dma((groups,)), dma((groups,)),
        ],
        compiler_params=pltpu.CompilerParams(
            collective_id=0, has_side_effects=True, vmem_limit_bytes=VMEM_BYTES
        ),
    )(pairs, count, extra, pairs, count, emb)

    halved = (2 * blocks, HALF, width)
    packed, index = pl.pallas_call(
        pack_kernel,
        out_shape=(
            shape(halved, jnp.bfloat16),
            shape((1, 1), jnp.int32),
        ),
        in_specs=[smem, smem, anyw, anyw],
        out_specs=(vmem, smem),
        scratch_shapes=[dma((2 * blocks,))],
        compiler_params=pltpu.CompilerParams(vmem_limit_bytes=VMEM_BYTES),
    )(need, peak, unit.reshape(halved), side.reshape(halved))

    def exchange(place, capacity):
        def run(packed, unit, mask):
            return pl.pallas_call(
                functools.partial(exchange_kernel, n, capacity),
                out_shape=(
                    shape((chips, 4 * blocks, HALF, width), jnp.bfloat16),
                    shape(blocks_shape, jnp.float32),
                    shape((blocks, BLOCK, LANES), jnp.float32),
                ),
                in_specs=[anyw, vmem, vmem],
                out_specs=(anyw, anyw, anyw),
                scratch_shapes=[
                    pltpu.VMEM(blocks_shape, jnp.float32),
                    pltpu.VMEM((blocks, BLOCK, LANES), jnp.float32),
                    dma((2,)),
                ] + [dma((chips, capacity)) for _ in range(4)],
                compiler_params=pltpu.CompilerParams(
                    collective_id=1 + place, has_side_effects=True, vmem_limit_bytes=VMEM_BYTES
                ),
            )(packed, unit, mask)

        return run

    branches = [exchange(i, c) for i, c in enumerate(capacities(blocks))]
    recv, acc, dens = lax.switch(index.reshape(()), branches, packed, unit, mask)

    entries = 2 * shifts * slots + 2
    centered, log_density = pl.pallas_call(
        functools.partial(far_kernel, n),
        out_shape=(
            shape(blocks_shape, jnp.bfloat16),
            shape((blocks, 1, BLOCK), jnp.float32),
        ),
        in_specs=[smem, smem, smem, smem, smem, vmem, anyw, anyw, anyw, anyw],
        out_specs=(anyw, vmem),
        scratch_shapes=[
            pltpu.VMEM(blocks_shape, jnp.bfloat16),
            dma((blocks,)),
            pltpu.VMEM(blocks_shape, jnp.float32),
            pltpu.VMEM((blocks, BLOCK, LANES), jnp.float32),
            pltpu.SMEM((entries,), jnp.int32),
            pltpu.SMEM((entries,), jnp.int32),
            pltpu.SMEM((n * blocks,), jnp.int32),
            pltpu.VMEM((DEPTH, BLOCK, width), jnp.bfloat16),
            dma((DEPTH,)),
            dma((2,)),
        ],
        compiler_params=pltpu.CompilerParams(vmem_limit_bytes=VMEM_BYTES),
    )(
        pairs, count, all_pairs, all_count, need, unit, acc, dens, side,
        recv.reshape(chips * 2 * blocks, BLOCK, width),
    )
    return (centered.reshape(-1, width), log_density.reshape(-1))


def solution(mesh):
    return jax.shard_map(
        shards,
        mesh=mesh,
        in_specs=(
            P(("group", "owner"), None),
            P("group", "owner", None, None, None),
            P("group", "owner", None),
            P("group", "owner", None, None),
        ),
        out_specs=(P(("group", "owner"), None), P(("group", "owner"))),
        check_vma=False,
    )
```
